32 devices in a mesh: dp: 8 (over z, core), tensor: 4 (over y, x).
Axes of the slice: x: 2, y: 2, z: 4, core: 2. Of those that a mesh axis runs over, the one named last changes fastest.
Arguments:
- tokens: bfloat16 [18432, 2048], P(('dp', 'tensor')), may hold values from -6 to 6
- cotangent: bfloat16 [18432, 2048], P(('dp', 'tensor')), may hold values from -6 to 6
- ln_gain: float32 [2048], replicated, may hold values from 0.5 to 1.5
- ln_bias: float32 [2048], replicated, may hold values from -3 to 3
- w_qkv: bfloat16 [3, 2048, 2048], P(None, 'dp', 'tensor')
- b_qkv: float32 [3, 2048], P(None, 'tensor'), may hold values from -3 to 3
- w_out: bfloat16 [2048, 2048], P('tensor', 'dp'), may hold values from -0.5 to 0.5
- w_fc1: bfloat16 [2048, 8192], P('dp', 'tensor'), may hold values from -0.125 to 0.125
- b_fc1: float32 [8192], P('tensor'), may hold values from -3 to 3
- w_fc2: bfloat16 [8192, 2048], P('tensor', 'dp'), may hold values from -0.0625 to 0.0625
- resid_bias: float32 [2048], replicated, may hold values from -3 to 3
- parents: int32 [8, 18], P('dp'), may hold values from 0 to 9, as said below
Outputs:
- output_rows: bfloat16 [18432, 2048], P(('dp', 'tensor'))
- input_grad: float32 [18432, 2048], P(('dp', 'tensor'))
- grad_small: float32 [3, 2048], P(None, ('dp', 'tensor'))
- grad_w_qkv: float32 [3, 2048, 2048], P(None, 'dp', 'tensor')
- grad_b_qkv: float32 [3, 2048], P(None, 'tensor')
- grad_w_out: float32 [2048, 2048], P('tensor', 'dp')
- grad_w_fc1: float32 [2048, 8192], P('dp', 'tensor')
- grad_b_fc1: float32 [8192], P('tensor')
- grad_w_fc2: float32 [8192, 2048], P('tensor', 'dp')
- clipped_qk: bfloat16 [2, 2048, 2048], P(None, 'dp', 'tensor')
The draws below stay inside these ranges and needn't reach their ends.
Inputs may be any that keep to these rules, and one draw needn't show every extreme that they name: `parents`: in each tree, segment 0 is its own parent and segment i < 6 has parent i - 1; the next 4 segments have parent 6 - 1; each of these is the parent of exactly 2 of the remaining segments.
All inputs are finite; a program needn't handle non-finite values.
Results may differ from the reference program's by a relative error of at most 0.014.
Values may be sent and summed in bfloat16 or wider, within the bound.
A program may use at most 384 MiB of HBM per device.

```python
import math
import jax
import jax.numpy as jnp
from jax import lax

D = 2048
HEADS = 32
HDIM = 64
ROT = 32
FF = 8192
SEG = 128
TRUNK = 6
BRANCHES = 4
LEAVES = 2
TREE = 2304
QBLK = 768
TREES = 8
TOKENS = 18432


def draw_w_qkv(key, part):
    scale_key, value_key = jax.random.split(key)
    head_scale = jnp.exp(jax.random.uniform(scale_key, (2, HEADS), jnp.float32, 0.0, math.log(1.7)))
    full_scale = jnp.concatenate([head_scale, jnp.ones((1, HEADS), jnp.float32)], axis=0)
    column_scale = jnp.repeat(full_scale, HDIM, axis=1)
    normal_part = jnp.clip(jax.random.normal(value_key, (3, D, HEADS * HDIM), jnp.float32), -6.0, 6.0)
    return (normal_part * column_scale[:, None, :] * D ** (-0.5)).astype(jnp.bfloat16)


def draw_parents(key, part):

    def one_tree(tree_key):
        trunk_ids = jnp.maximum(jnp.arange(TRUNK, dtype=jnp.int32) - 1, 0)
        branch_ids = jnp.full((BRANCHES,), TRUNK - 1, jnp.int32)
        leaf_ids = jax.random.permutation(tree_key, jnp.repeat(jnp.arange(TRUNK, TRUNK + BRANCHES, dtype=jnp.int32), LEAVES))
        return jnp.concatenate([trunk_ids, branch_ids, leaf_ids]).astype(jnp.int32)
    return jax.vmap(one_tree)(jax.random.split(key, TREES))


def block_levels(stream_key, dims, pieces, smallest, high):
    factor_of, own = 1.0, jax.random.fold_in(stream_key, 6)
    for position, shards_of in pieces:
        draws = jnp.exp(jax.random.uniform(jax.random.fold_in(own, position), (shards_of,), jnp.float32, smallest / len(pieces), high / len(pieces)))
        factor_of = factor_of * jnp.repeat(draws, dims[position] // shards_of).reshape([-1 if axis == position else 1 for axis in range(len(dims))])
    return factor_of


def bell_draw(key, extent, width, most, pieces=(), kind=jnp.bfloat16):
    values = width * jax.random.normal(key, extent, jnp.float32)
    if pieces:
        values = values * block_levels(key, extent, pieces, -0.22, 0.18)
    return jnp.clip(values, -most, most).astype(kind)


def setup_inputs(seed: int = 0) -> dict:
    seeds = jax.random.split(jax.random.key(seed), 13)
    tokens = bell_draw(seeds[0], (TOKENS, D), 1.0, 6.0, ((0, 32),))
    cotangent = bell_draw(seeds[1], (TOKENS, D), 1.0, 6.0, ((0, 32),))
    ln_gain = jnp.clip(1.0 + 0.1 * jax.random.normal(seeds[2], (D,), jnp.float32), 0.5, 1.5)
    ln_bias = bell_draw(seeds[3], (D,), 0.3, 3.0, (), jnp.float32)
    w_qkv = draw_w_qkv(jax.random.fold_in(seeds[12], 71), 0)
    b_qkv = bell_draw(seeds[5], (3, HEADS * HDIM), 0.3, 3.0, ((1, 4),), jnp.float32)
    w_out = bell_draw(seeds[6], (HEADS * HDIM, D), (HEADS * HDIM // 16) ** -0.5, 0.5, ((0, 4), (1, 8)))
    w_fc1 = bell_draw(seeds[7], (D, FF), D ** -0.5, 0.125, ((0, 8), (1, 4)))
    b_fc1 = bell_draw(seeds[8], (FF,), 0.5, 3.0, ((0, 4),), jnp.float32)
    w_fc2 = bell_draw(seeds[9], (FF, D), FF ** -0.5, 0.0625, ((0, 4), (1, 8)))
    resid_bias = bell_draw(seeds[10], (D,), 0.3, 3.0, (), jnp.float32)
    parents = draw_parents(jax.random.fold_in(seeds[12], 71), 0)
    return {"tokens": tokens, "cotangent": cotangent, "ln_gain": ln_gain, "ln_bias": ln_bias, "w_qkv": w_qkv, "b_qkv": b_qkv, "w_out": w_out, "w_fc1": w_fc1, "b_fc1": b_fc1, "w_fc2": w_fc2, "resid_bias": resid_bias, "parents": parents}


clip_tau = 10.0
norm_eps = 1e-05
rope_base = 10000.0
highest = lax.Precision.HIGHEST

@jax.custom_vjp
def low(v):
    return lax.optimization_barrier(v.astype(jnp.bfloat16)).astype(jnp.float32)

@jax.custom_vjp
def low_back(v):
    return v

def low_keep(v):
    return (low(v), None)

def low_pass(kept, grad):
    return (grad,)

def back_keep(v):
    return (v, None)

def back_low(kept, grad):
    return (low(grad),)
low.defvjp(low_keep, low_pass)
low_back.defvjp(back_keep, back_low)

def tree_layout(parent_ids, seg_len):
    seg_count = parent_ids.shape[0]
    labels = jnp.arange(seg_count, dtype=jnp.int32)
    current = labels
    depth_seg = jnp.zeros((seg_count,), jnp.int32)
    ancestry = labels[:, None] == labels[None, :]
    for step_index in range(seg_count):
        depth_seg = depth_seg + (current != 0).astype(jnp.int32)
        current = lax.optimization_barrier(jnp.sum(jnp.where(current[:, None] == labels[None, :], parent_ids[None, :], 0), axis=1)).astype(jnp.int32)
        ancestry = ancestry | (current[:, None] == labels[None, :])
    positions = jnp.repeat(depth_seg, seg_len) * seg_len + jnp.tile(jnp.arange(seg_len, dtype=jnp.int32), seg_count)
    return (positions, ancestry)

def rotary_tables(positions):
    half_rot = ROT // 2
    inverse_freq = 1.0 / rope_base ** (jnp.arange(half_rot, dtype=jnp.float32) * (2.0 / ROT))
    angles = positions.astype(jnp.float32)[:, None] * inverse_freq[None, :]
    return (jnp.cos(angles), jnp.sin(angles))

def rotate(block_in, cos_rows, sin_rows):
    half_rot = ROT // 2
    first_half = block_in[..., :half_rot]
    second_half = block_in[..., half_rot:ROT]
    cos_heads = cos_rows[:, None, :]
    sin_heads = sin_rows[:, None, :]
    return jnp.concatenate([first_half * cos_heads - second_half * sin_heads, second_half * cos_heads + first_half * sin_heads, block_in[..., ROT:]], axis=-1)

def block_mask(ancestry, row_start, row_count, total_rows, seg_len):
    row_ids = row_start + jnp.arange(row_count, dtype=jnp.int32)
    col_ids = jnp.arange(total_rows, dtype=jnp.int32)
    seg_rows = lax.dynamic_slice_in_dim(ancestry, row_start // seg_len, row_count // seg_len, 0)
    widened = jnp.repeat(jnp.repeat(seg_rows, seg_len, axis=0), seg_len, axis=1)
    same_seg = row_ids[:, None] // seg_len == col_ids[None, :] // seg_len
    return widened & (~same_seg | (col_ids[None, :] <= row_ids[:, None]))

def norm_rows(rows_in, gain_in, shift_in):
    row_mean = lax.optimization_barrier(jnp.mean(rows_in, axis=-1, keepdims=True))
    centred = rows_in - row_mean
    inverse = lax.rsqrt(lax.optimization_barrier(jnp.mean(centred * centred, axis=-1, keepdims=True)) + norm_eps)
    return centred * inverse * gain_in + shift_in

def tree_forward(rows_in, parent_ids, ln_gain, ln_bias, qkv_w, b_qkv, out_w, up_w, b_fc1, down_w, resid_bias):
    positions, ancestry = tree_layout(parent_ids, SEG)
    cos_rows, sin_rows = rotary_tables(positions)
    normed = low(norm_rows(rows_in, ln_gain, ln_bias))
    projected = low_back(jnp.einsum('td,cdh->cth', normed, qkv_w, precision=highest) + b_qkv[:, None, :])
    heads_view = projected.reshape(3, TREE, HEADS, HDIM)
    queries = low(rotate(heads_view[0], cos_rows, sin_rows))
    keys_rot = low(rotate(heads_view[1], cos_rows, sin_rows))
    values_all = low(heads_view[2])
    score_scale = HDIM ** (-0.5)

    def attend_block(row_start):
        query_rows = lax.dynamic_slice_in_dim(queries, row_start, QBLK, 0)
        raw_scores = low_back(jnp.einsum('qhe,khe->hqk', query_rows, keys_rot, precision=highest) * score_scale)
        allowed = block_mask(ancestry, row_start, QBLK, TREE, SEG)
        masked = jnp.where(allowed[None], raw_scores, -1e+30)
        row_top = lax.optimization_barrier(jnp.max(masked, axis=2, keepdims=True))
        exponent = jnp.exp(masked - row_top)
        probs_low = low(exponent / lax.optimization_barrier(jnp.sum(exponent, axis=2, keepdims=True)))
        attended = jnp.einsum('hqk,khe->qhe', probs_low, values_all, precision=highest)
        return (attended, lax.optimization_barrier(jnp.max(row_top[..., 0], axis=1)))
    block_starts = jnp.arange(TREE // QBLK, dtype=jnp.int32) * QBLK
    attended, block_tops = lax.map(jax.checkpoint(attend_block), block_starts)
    attended = low_back(low(attended.reshape(TREE, HEADS * HDIM)))
    hidden_pre = low_back(jnp.dot(normed, up_w, precision=highest) + b_fc1)
    activated = low(jax.nn.gelu(hidden_pre, approximate=True))
    result = rows_in + jnp.dot(attended, out_w, precision=highest) + jnp.dot(activated, down_w, precision=highest) + resid_bias
    return (result, lax.optimization_barrier(jnp.max(block_tops, axis=0)))

def reference(tokens, cotangent, ln_gain, ln_bias, w_qkv, b_qkv, w_out, w_fc1, b_fc1, w_fc2, resid_bias, parents):
    rows_all = tokens.astype(jnp.float32).reshape(TREES, TREE, D)

    def forward(rows_in, gain_in, shift_in, qkv_w, qkv_bias, out_w, up_w, up_bias, down_w, extra_bias):

        def one_tree(tree_pair):
            return tree_forward(tree_pair[0], tree_pair[1], gain_in, shift_in, qkv_w, qkv_bias, out_w, up_w, up_bias, down_w, extra_bias)
        return lax.map(one_tree, (rows_in, parents))
    tree_outs, pullback, tree_tops = jax.vjp(forward, rows_all, ln_gain, ln_bias, w_qkv.astype(jnp.float32), b_qkv, w_out.astype(jnp.float32), w_fc1.astype(jnp.float32), b_fc1, w_fc2.astype(jnp.float32), resid_bias, has_aux=True)
    gradients = pullback(cotangent.astype(jnp.float32).reshape(TREES, TREE, D))
    grad_rows, grad_gain, grad_shift, grad_w_qkv, grad_b_qkv, grad_w_out, grad_w_fc1, grad_b_fc1, grad_w_fc2, grad_extra = gradients
    output_rows = tree_outs.reshape(TOKENS, D).astype(jnp.bfloat16)
    input_grad = grad_rows.reshape(TOKENS, D)
    grad_small = jnp.stack([grad_gain, grad_shift, grad_extra])
    head_top = lax.optimization_barrier(jnp.max(tree_tops, axis=0))
    factor = jnp.sqrt(clip_tau / jnp.maximum(head_top, clip_tau))
    clipped_qk = (w_qkv[:2].astype(jnp.float32) * jnp.repeat(factor, HDIM)[None, None, :]).astype(jnp.bfloat16)
    return (output_rows, input_grad, grad_small, grad_w_qkv, grad_b_qkv, grad_w_out, grad_w_fc1, grad_b_fc1, grad_w_fc2, clipped_qk)
```

```python
import jax
import jax.numpy as jnp
from jax import lax
from jax.experimental import pallas as pl
from jax.experimental.pallas import tpu as pltpu
from jax.sharding import PartitionSpec as P

HDIM = 64
ROT = 32
SEG = 128
TRUNK = 6
BRANCHES = 4
LEAVES = 2
TREE_SEGS = TRUNK + BRANCHES + BRANCHES * LEAVES
bf16 = jnp.bfloat16
f32 = jnp.float32
NEG = -1e30
rope_base = 10000.0


def dot_nn(a, b):
    return lax.dot_general(a, b, (((1,), (0,)), ((), ())), preferred_element_type=f32)


def dot_nt(a, b):
    return lax.dot_general(a, b, (((1,), (1,)), ((), ())), preferred_element_type=f32)


def rope_tables():
    seg = jnp.arange(TREE_SEGS, dtype=jnp.int32)
    depth = jnp.where(seg < TRUNK, seg, jnp.where(seg < TRUNK + BRANCHES, TRUNK, TRUNK + 1))
    pos = (depth[:, None] * SEG + jnp.arange(SEG, dtype=jnp.int32)[None, :]).reshape(-1)
    half = ROT // 2
    inverse_freq = 1.0 / rope_base ** (jnp.arange(half, dtype=f32) * (2.0 / ROT))
    angles = pos.astype(f32)[:, None] * inverse_freq[None, :]
    cos, sin = jnp.cos(angles), jnp.sin(angles)
    rows = pos.shape[0]
    ones = jnp.ones((rows, HDIM - ROT), f32)
    cos_h = jnp.concatenate([cos, cos, ones], axis=1)
    sin_h = jnp.concatenate([-sin, sin, 0.0 * ones], axis=1)
    return jnp.concatenate([cos_h, cos_h], axis=1), jnp.concatenate([sin_h, sin_h], axis=1)


def partner(x):
    lane = lax.broadcasted_iota(jnp.int32, x.shape, 1) % HDIM
    half = ROT // 2
    return jnp.where(lane < half, pltpu.roll(x, 2 * HDIM - half, 1), pltpu.roll(x, half, 1))


def attn_kernel(par, cos_ref, sin_ref, qkv_ref, do_ref, att_ref, g_ref, aux_ref,
                qs, kr, kt, vt, ot, dqt, dk, dv, s_ref, p_ref, top):
    rows = TREE_SEGS * SEG
    step = 2 * SEG
    lane_low = lax.broadcasted_iota(jnp.int32, (step, 2 * HDIM), 1) < HDIM

    @pl.loop(0, rows // step)
    def _(i):
        at = pl.ds(pl.multiple_of(i * step, step), step)
        cos, sin = cos_ref[at, :], sin_ref[at, :]
        q = qkv_ref[0, at, :].astype(f32)
        k = qkv_ref[1, at, :].astype(f32)
        v = qkv_ref[2, at, :].astype(f32)
        qs[at, :] = ((q * cos + partner(q) * sin) * (HDIM ** -0.5)).astype(bf16)
        k = k * cos + partner(k) * sin
        kr[at, :] = k.astype(bf16)
        kt[:, at] = k.T.astype(bf16)
        vt[:, at] = v.T.astype(bf16)
        dk[at, :] = jnp.zeros((step, 2 * HDIM), f32)
        dv[at, :] = jnp.zeros((step, 2 * HDIM), f32)

    top[...] = jnp.full((2, 8, step), NEG, f32)
    key_id = lax.broadcasted_iota(jnp.int32, (SEG, step), 0)
    query_id = lax.broadcasted_iota(jnp.int32, (SEG, step), 1) % SEG
    pair_mask = key_id <= query_id
    tri_mask = lax.broadcasted_iota(jnp.int32, (step, step), 0) <= lax.broadcasted_iota(
        jnp.int32, (step, step), 1)

    def seg_at(start, size):
        if isinstance(start, int):
            return pl.ds(start, size)
        return pl.ds(pl.multiple_of(start, SEG), size)

    def block(q0, q1, chunks, diag):
        halves = [seg_at(q0, SEG), seg_at(q1, SEG)]
        q_all = jnp.concatenate([qs[halves[0], :], qs[halves[1], :]], axis=0)
        do_all = jnp.concatenate([do_ref[halves[0], :], do_ref[halves[1], :]], axis=0)
        zero = jnp.zeros_like(q_all)
        pieces = []
        off = 0
        for start, size in chunks:
            pieces.append((off, start, size, 'full'))
            off += size
        if diag:
            pieces.append((off, q0, step, 'tri'))
            off += step
        else:
            pieces.append((off, None, SEG, 'pair'))
            off += SEG
        for h in range(2):
            qh = jnp.where(lane_low if h == 0 else ~lane_low, q_all, zero)
            dh = jnp.where(lane_low if h == 0 else ~lane_low, do_all, zero)

            def left(ref, piece, rhs):
                o, start, size, kind = piece
                if kind == 'pair':
                    return jnp.concatenate(
                        [dot_nt(ref[halves[i], :], rhs[i * SEG:(i + 1) * SEG]) for i in range(2)], axis=1)
                return dot_nt(ref[seg_at(start, size), :], rhs)

            m = None
            for piece in pieces:
                o, start, size, kind = piece
                s = left(kr, piece, qh)
                if kind == 'tri':
                    s = jnp.where(tri_mask, s, NEG)
                if kind == 'pair':
                    s = jnp.where(pair_mask, s, NEG)
                s_ref[h, o:o + size, :] = s
                mp = jnp.max(s.reshape(size // 8, 8, step), axis=0)
                m = mp if m is None else jnp.maximum(m, mp)
            top[h] = jnp.maximum(top[h], m)
            m = jnp.max(m, axis=0, keepdims=True)
            total = jnp.zeros((8, step), f32)
            for o, start, size, kind in pieces:
                e = jnp.exp(s_ref[h, o:o + size, :] - m)
                s_ref[h, o:o + size, :] = e
                total = total + jnp.sum(e.reshape(size // 8, 8, step), axis=0)
            inv = 1.0 / jnp.sum(total, axis=0, keepdims=True)
            delta = jnp.zeros((8, step), f32)
            o_acc = jnp.zeros((HDIM, step), f32)
            for piece in pieces:
                o, start, size, kind = piece
                p = s_ref[h, o:o + size, :] * inv
                pb = p.astype(bf16)
                if kind == 'pair':
                    o_acc = o_acc + jnp.concatenate(
                        [dot_nn(vt[h * HDIM:(h + 1) * HDIM, halves[i]], pb[:, i * SEG:(i + 1) * SEG])
                         for i in range(2)], axis=1)
                    for i in range(2):
                        dv[halves[i], :] += dot_nn(pb[:, i * SEG:(i + 1) * SEG], dh[i * SEG:(i + 1) * SEG])
                else:
                    at = seg_at(start, size)
                    o_acc = o_acc + dot_nn(vt[h * HDIM:(h + 1) * HDIM, at], pb)
                    dv[at, :] += dot_nn(pb, dh)
                s_ref[h, o:o + size, :] = p
                dp = left_v(piece, dh, halves)
                p_ref[h, o:o + size, :] = dp
                delta = delta + jnp.sum((p * dp).reshape(size // 8, 8, step), axis=0)
            delta = jnp.sum(delta, axis=0, keepdims=True)
            dq_acc = jnp.zeros((HDIM, step), f32)
            for piece in pieces:
                o, start, size, kind = piece
                ds = (s_ref[h, o:o + size, :] * (p_ref[h, o:o + size, :] - delta)).astype(bf16)
                if kind == 'pair':
                    dq_acc = dq_acc + jnp.concatenate(
                        [dot_nn(kt[h * HDIM:(h + 1) * HDIM, halves[i]], ds[:, i * SEG:(i + 1) * SEG])
                         for i in range(2)], axis=1)
                    for i in range(2):
                        dk[halves[i], :] += dot_nn(ds[:, i * SEG:(i + 1) * SEG], qh[i * SEG:(i + 1) * SEG])
                else:
                    at = seg_at(start, size)
                    dq_acc = dq_acc + dot_nn(kt[h * HDIM:(h + 1) * HDIM, at], ds)
                    dk[at, :] += dot_nn(ds, qh)
            for i in range(2):
                ot[h * HDIM:(h + 1) * HDIM, halves[i]] = o_acc[:, i * SEG:(i + 1) * SEG]
                dqt[h * HDIM:(h + 1) * HDIM, halves[i]] = dq_acc[:, i * SEG:(i + 1) * SEG]

    def left_v(piece, rhs, halves):
        o, start, size, kind = piece
        if kind == 'pair':
            return jnp.concatenate(
                [dot_nt(qkv_ref[2, halves[i], :], rhs[i * SEG:(i + 1) * SEG]) for i in range(2)], axis=1)
        return dot_nt(qkv_ref[2, seg_at(start, size), :], rhs)

    for b in range(TRUNK // 2):
        block(b * step, b * step + SEG, [(c * step, step) for c in range(b)], True)
    trunk_chunks = [(c * step, step) for c in range(TRUNK // 2)]

    @pl.loop(0, BRANCHES // 2)
    def _(i):
        start = (TRUNK + 2 * i) * SEG
        block(start, start + SEG, trunk_chunks, False)

    @pl.loop(0, BRANCHES)
    def _(i):
        branch = TRUNK + i
        first = TREE_SEGS - 1
        last = TRUNK + BRANCHES
        for leaf in range(TREE_SEGS - 1, TRUNK + BRANCHES - 1, -1):
            first = jnp.where(par[leaf] == branch, leaf, first)
        for leaf in range(TRUNK + BRANCHES, TREE_SEGS):
            last = jnp.where(par[leaf] == branch, leaf, last)
        block(first * SEG, last * SEG, trunk_chunks + [(branch * SEG, SEG)], False)

    sums = [jnp.zeros((8, 2 * HDIM), f32)] * 3

    @pl.loop(0, rows // step, init_carry=tuple(sums))
    def totals(i, carry):
        at = pl.ds(pl.multiple_of(i * step, step), step)
        cos, sin = cos_ref[at, :], sin_ref[at, :]
        att_ref[at, :] = ot[:, at].T.astype(bf16)
        dq = dqt[:, at].T * (HDIM ** -0.5)
        dkr = dk[at, :]
        parts = [dq * cos - partner(dq) * sin, dkr * cos - partner(dkr) * sin, dv[at, :]]
        out = []
        for c in range(3):
            low = parts[c].astype(bf16)
            g_ref[c, at, :] = low
            out.append(carry[c] + jnp.sum(low.astype(f32).reshape(step // 8, 8, 2 * HDIM), axis=0))
        return tuple(out)

    rows_out = [jnp.sum(t, axis=0, keepdims=True) for t in totals]
    for h in range(2):
        rows_out.append(jnp.full((1, 2 * HDIM), jnp.max(top[h]), f32))
    rows_out.append(jnp.zeros((3, 2 * HDIM), f32))
    aux_ref[0] = jnp.concatenate(rows_out, axis=0)


def attention(parents, cos, sin, qkv, grad_att):
    rows, width = grad_att.shape
    pairs = width // (2 * HDIM)
    step = 2 * SEG
    wide = 2 * HDIM
    keys = TRUNK * SEG + 2 * SEG
    blk = lambda: pl.BlockSpec((rows, wide), lambda p, par: (0, p))
    blk3 = lambda: pl.BlockSpec((3, rows, wide), lambda p, par: (0, 0, p))
    tab = lambda: pl.BlockSpec((rows, wide), lambda p, par: (0, 0))
    return pl.pallas_call(
        attn_kernel,
        out_shape=(
            jax.ShapeDtypeStruct((rows, width), bf16),
            jax.ShapeDtypeStruct((3, rows, width), bf16),
            jax.ShapeDtypeStruct((pairs, 8, wide), f32),
        ),
        grid_spec=pltpu.PrefetchScalarGridSpec(
            num_scalar_prefetch=1,
            grid=(pairs,),
            in_specs=[tab(), tab(), blk3(), blk()],
            out_specs=[blk(), blk3(), pl.BlockSpec((1, 8, wide), lambda p, par: (p, 0, 0))],
            scratch_shapes=[
                pltpu.VMEM((rows, wide), bf16),
                pltpu.VMEM((rows, wide), bf16),
                pltpu.VMEM((wide, rows), bf16),
                pltpu.VMEM((wide, rows), bf16),
                pltpu.VMEM((wide, rows), f32),
                pltpu.VMEM((wide, rows), f32),
                pltpu.VMEM((rows, wide), f32),
                pltpu.VMEM((rows, wide), f32),
                pltpu.VMEM((2, keys, step), f32),
                pltpu.VMEM((2, keys, step), f32),
                pltpu.VMEM((2, 8, step), f32),
            ],
        ),
        compiler_params=pltpu.CompilerParams(
            dimension_semantics=("arbitrary",), vmem_limit_bytes=40 << 20),
        cost_estimate=pl.CostEstimate(flops=60 * 10**9, transcendentals=17 * 10**6, bytes_accessed=24 << 20),
    )(parents, cos, sin, qkv, grad_att)


clip_tau = 10.0
norm_eps = 1e-05


def dot_tn(a, b):
    return lax.dot_general(a, b, (((0,), (0,)), ((), ())), preferred_element_type=f32)


def xor_send(x, bits, size):
    return lax.ppermute(x, "tensor", [(i, i ^ bits) for i in range(size)])


def gather_rows(x, size):
    if size != 4:
        return [x] + [xor_send(x, i, size) for i in range(1, size)]
    half = x.shape[0] // 2
    one = xor_send(x, 1, size)
    two = xor_send(x, 2, size)
    low = xor_send(two[:half], 1, size)
    high = xor_send(one[half:], 2, size)
    return [x, one, two, jnp.concatenate([low, high], axis=0)]


def scatter_sum(parts, size):
    total = parts[0].astype(f32)
    if size != 4:
        for i in range(1, size):
            total = total + xor_send(parts[i], i, size).astype(f32)
        return total
    half = parts[0].shape[0] // 2
    low = xor_send(parts[3][:half], 1, size)
    high = xor_send(parts[3][half:], 2, size)
    two = jnp.concatenate(
        [(parts[2][:half].astype(f32) + low.astype(f32)).astype(bf16), parts[2][half:]], axis=0)
    one = jnp.concatenate(
        [parts[1][:half], (parts[1][half:].astype(f32) + high.astype(f32)).astype(bf16)], axis=0)
    return total + xor_send(one, 1, size).astype(f32) + xor_send(two, 2, size).astype(f32)


def norm_parts(rows_in):
    row_mean = jnp.mean(rows_in, axis=-1, keepdims=True)
    centred = rows_in - row_mean
    inverse = lax.rsqrt(jnp.mean(centred * centred, axis=-1, keepdims=True) + norm_eps)
    return centred * inverse, inverse


def gelu_tanh(values_in):
    return jax.nn.gelu(values_in, approximate=True)


def body(
    tokens,
    cotangent,
    ln_gain,
    ln_bias,
    w_qkv,
    b_qkv,
    w_out,
    w_fc1,
    b_fc1,
    w_fc2,
    resid_bias,
    parents,
):
    size = lax.axis_size("tensor")
    groups = lax.axis_size("dp")
    local_rows, model = tokens.shape
    total_rows = local_rows * size
    me = lax.axis_index("tensor")
    width = w_qkv.shape[2]
    heads = width // HDIM

    def to_tree(parts):
        out = jnp.zeros((total_rows,) + parts[0].shape[1:], parts[0].dtype)
        for i, part in enumerate(parts):
            out = lax.dynamic_update_slice_in_dim(out, part, (me ^ i) * local_rows, 0)
        return out

    def from_tree(x):
        return [
            lax.dynamic_slice_in_dim(x, (me ^ i) * local_rows, local_rows, 0) for i in range(size)
        ]

    cos, sin = rope_tables()
    tokens_f = tokens.astype(f32)
    xhat, inverse = norm_parts(tokens_f)
    normed_local = (xhat * ln_gain + ln_bias).astype(bf16)
    qkv_w = lax.all_gather(w_qkv, "dp", axis=1, tiled=True)
    out_w = lax.all_gather(w_out, "dp", axis=1, tiled=True)
    up_w = lax.all_gather(w_fc1, "dp", axis=0, tiled=True)
    down_w = lax.all_gather(w_fc2, "dp", axis=1, tiled=True)
    normed = to_tree(gather_rows(normed_local, size))
    cot_full = to_tree(gather_rows(cotangent, size))

    projected = (
        jnp.einsum("td,cdh->cth", normed, qkv_w, preferred_element_type=f32) + b_qkv[:, None, :]
    ).astype(bf16)
    grad_attended = dot_nt(cot_full, out_w).astype(bf16)
    attended, grad_qkv, aux = attention(parents[0], cos, sin, projected, grad_attended)
    grad_b_qkv = jnp.transpose(aux[:, :3], (1, 0, 2)).reshape(-1)
    tops = aux[:, 3:5, 0].reshape(-1)

    hidden_pre = dot_nn(normed, up_w) + b_fc1
    activated = gelu_tanh(hidden_pre).astype(bf16)
    hidden_low = hidden_pre.astype(bf16)
    grad_w_out = dot_tn(attended, cot_full).astype(bf16)
    grad_w_qkv = jnp.einsum("td,cth->cdh", normed, grad_qkv, preferred_element_type=f32).astype(bf16)
    grad_w_fc2 = dot_tn(activated, cot_full).astype(bf16)
    branch = (dot_nn(attended, out_w) + dot_nn(activated, down_w)).astype(bf16)
    grad_act = dot_nt(cot_full, down_w)
    ignored, gelu_back = jax.vjp(gelu_tanh, hidden_low.astype(f32))
    grad_hidden = gelu_back(grad_act)[0].astype(bf16)
    grad_w_fc1 = dot_tn(normed, grad_hidden).astype(bf16)
    grad_b_fc1 = jnp.sum(grad_hidden.astype(f32), axis=0)
    normed_part = (
        jnp.einsum("cth,cdh->td", grad_qkv, qkv_w, preferred_element_type=f32)
        + dot_nt(grad_hidden, up_w)
    ).astype(bf16)

    summed_fc2 = lax.psum_scatter(grad_w_fc2, "dp", scatter_dimension=1, tiled=True).astype(f32)
    summed_qkv = lax.psum_scatter(grad_w_qkv, "dp", scatter_dimension=1, tiled=True).astype(f32)
    summed_out = lax.psum_scatter(grad_w_out, "dp", scatter_dimension=1, tiled=True).astype(f32)
    summed_fc1 = lax.psum_scatter(grad_w_fc1, "dp", scatter_dimension=0, tiled=True).astype(f32)

    branch_sum = scatter_sum(from_tree(branch), size)
    output_rows = (tokens_f + branch_sum + resid_bias).astype(bf16)

    small = jnp.concatenate([grad_b_qkv, grad_b_fc1, tops])
    small_all = lax.all_gather(small[None], "dp", axis=0, tiled=True)
    small_sum = jnp.sum(small_all[:, : -heads], axis=0)
    bias_qkv = small_sum[: 3 * width].reshape(3, width)
    bias_fc1 = small_sum[3 * width :]
    head_top = jnp.max(small_all[:, -heads:], axis=0)
    factor = jnp.sqrt(clip_tau / jnp.maximum(head_top, clip_tau))
    clipped_qk = (w_qkv[:2].astype(f32) * jnp.repeat(factor, HDIM)[None, None, :]).astype(bf16)

    grad_normed = scatter_sum(from_tree(normed_part), size)
    grad_xhat = grad_normed * ln_gain
    cot_local = cotangent.astype(f32)
    input_grad = cot_local + inverse * (
        grad_xhat
        - jnp.mean(grad_xhat, axis=-1, keepdims=True)
        - xhat * jnp.mean(grad_xhat * xhat, axis=-1, keepdims=True)
    )
    terms = jnp.stack(
        [jnp.sum(grad_normed * xhat, axis=0), jnp.sum(grad_normed, axis=0), jnp.sum(cot_local, axis=0)]
    )
    every = size * groups
    pieces = jnp.transpose(terms.reshape(3, every, model // every), (1, 0, 2)).reshape(every, -1)
    pieces = lax.all_to_all(pieces, ("dp", "tensor"), 0, 0, tiled=True)
    grad_small = jnp.sum(pieces, axis=0).reshape(3, model // every)
    return (
        output_rows,
        input_grad,
        grad_small,
        summed_qkv,
        bias_qkv,
        summed_out,
        summed_fc1,
        bias_fc1,
        summed_fc2,
        clipped_qk,
    )


def solution(mesh):
    return jax.shard_map(
        body,
        mesh=mesh,
        in_specs=(
            P(("dp", "tensor"), None),
            P(("dp", "tensor"), None),
            P(),
            P(),
            P(None, "dp", "tensor"),
            P(None, "tensor"),
            P("tensor", "dp"),
            P("dp", "tensor"),
            P("tensor"),
            P("tensor", "dp"),
            P(),
            P("dp", None),
        ),
        out_specs=(
            P(("dp", "tensor"), None),
            P(("dp", "tensor"), None),
            P(None, ("dp", "tensor")),
            P(None, "dp", "tensor"),
            P(None, "tensor"),
            P("tensor", "dp"),
            P("dp", "tensor"),
            P("tensor"),
            P("tensor", "dp"),
            P(None, "dp", "tensor"),
        ),
        check_vma=False,
    )
```

```python
import functools

import jax
import jax.numpy as jnp
from jax import lax
from jax.experimental import pallas as pl
from jax.experimental.pallas import tpu as pltpu
from jax.sharding import PartitionSpec as P

HDIM = 64
ROT = 32
SEG = 128
TRUNK = 6
BRANCHES = 4
LEAVES = 2
TREE_SEGS = TRUNK + BRANCHES + BRANCHES * LEAVES
bf16 = jnp.bfloat16
f32 = jnp.float32
NEG = -1e30
rope_base = 10000.0


def dot_nn(a, b):
    return lax.dot_general(a, b, (((1,), (0,)), ((), ())), preferred_element_type=f32)


def dot_nt(a, b):
    return lax.dot_general(a, b, (((1,), (1,)), ((), ())), preferred_element_type=f32)


def rope_tables():
    seg = jnp.arange(TREE_SEGS, dtype=jnp.int32)
    depth = jnp.where(seg < TRUNK, seg, jnp.where(seg < TRUNK + BRANCHES, TRUNK, TRUNK + 1))
    pos = (depth[:, None] * SEG + jnp.arange(SEG, dtype=jnp.int32)[None, :]).reshape(-1)
    half = ROT // 2
    inverse_freq = 1.0 / rope_base ** (jnp.arange(half, dtype=f32) * (2.0 / ROT))
    angles = pos.astype(f32)[:, None] * inverse_freq[None, :]
    cos, sin = jnp.cos(angles), jnp.sin(angles)
    rows = pos.shape[0]
    ones = jnp.ones((rows, HDIM - ROT), f32)
    cos_h = jnp.concatenate([cos, cos, ones], axis=1)
    sin_h = jnp.concatenate([-sin, sin, 0.0 * ones], axis=1)
    return jnp.concatenate([cos_h, cos_h], axis=1), jnp.concatenate([sin_h, sin_h], axis=1)


def partner(x):
    lane = lax.broadcasted_iota(jnp.int32, x.shape, 1) % HDIM
    half = ROT // 2
    return jnp.where(lane < half, pltpu.roll(x, 2 * HDIM - half, 1), pltpu.roll(x, half, 1))


def attn_kernel(size, par, me, cos_ref, sin_ref, qkv_ref, do_in, att_ref, g_ref, aux_ref,
                qs, kr, vr, do_ref, kt, vt, dot_t, att, dqn, dk, dv, s_ref, top):
    rows = TREE_SEGS * SEG
    step = 2 * SEG
    local = rows // size
    lane_low = lax.broadcasted_iota(jnp.int32, (step, 2 * HDIM), 1) < HDIM

    def unit(n):
        return jnp.where(
            lax.broadcasted_iota(jnp.int32, (n, n), 0) == lax.broadcasted_iota(jnp.int32, (n, n), 1),
            1.0, 0.0).astype(bf16)

    unit_wide = unit(2 * HDIM)

    def places(i):
        here = pl.ds(i * local, local)
        there = pl.ds(pl.multiple_of((me[0] ^ i) * local, local), local)
        return here, there

    for i in range(size):
        here, there = places(i)
        cos, sin = cos_ref[there, :], sin_ref[there, :]
        q = qkv_ref[0, here, :].astype(f32)
        k = qkv_ref[1, here, :].astype(f32)
        qs[there, :] = ((q * cos + partner(q) * sin) * (HDIM ** -0.5)).astype(bf16)
        kr[there, :] = (k * cos + partner(k) * sin).astype(bf16)
        vr[there, :] = qkv_ref[2, here, :]
        do_ref[there, :] = do_in[here, :]

    for i in range(rows // step):
        at = pl.ds(i * step, step)
        kt[:, at] = dot_nt(unit_wide, kr[at, :]).astype(bf16)
        vt[:, at] = dot_nt(unit_wide, vr[at, :]).astype(bf16)
        dot_t[:, at] = dot_nt(unit_wide, do_ref[at, :]).astype(bf16)
        dk[at, :] = jnp.zeros((step, 2 * HDIM), f32)
        dv[at, :] = jnp.zeros((step, 2 * HDIM), f32)

    top[...] = jnp.full((2, 8, step), NEG, f32)
    key_id = lax.broadcasted_iota(jnp.int32, (SEG, step), 0)
    query_id = lax.broadcasted_iota(jnp.int32, (SEG, step), 1) % SEG
    pair_mask = key_id <= query_id
    tri_mask = lax.broadcasted_iota(jnp.int32, (step, step), 0) <= lax.broadcasted_iota(
        jnp.int32, (step, step), 1)

    def seg_at(start, size):
        if isinstance(start, int):
            return pl.ds(start, size)
        return pl.ds(pl.multiple_of(start, SEG), size)

    def block(q0, q1, chunks, diag):
        halves = [seg_at(q0, SEG), seg_at(q1, SEG)]
        q_all = jnp.concatenate([qs[halves[0], :], qs[halves[1], :]], axis=0)
        do_all = jnp.concatenate([do_ref[halves[0], :], do_ref[halves[1], :]], axis=0)
        zero = jnp.zeros_like(q_all)
        pieces = []
        off = 0
        for start, size in chunks:
            pieces.append((off, start, size, 'full'))
            off += size
        pieces.append((off, q0, step, 'tri') if diag else (off, None, SEG, 'pair'))
        both = range(2)
        qh = [jnp.where(lane_low if h == 0 else ~lane_low, q_all, zero) for h in both]
        dh = [jnp.where(lane_low if h == 0 else ~lane_low, do_all, zero) for h in both]
        q_stack = jnp.concatenate(qh, axis=0)
        d_stack = jnp.concatenate(dh, axis=0)

        def part(x, i):
            return x[i * SEG:(i + 1) * SEG]

        def lanes(x, i):
            return x[:, i * SEG:(i + 1) * SEG]

        def left(ref, piece, rhs):
            o, start, size, kind = piece
            if kind == 'pair':
                return jnp.concatenate(
                    [dot_nt(ref[halves[i], :], part(rhs, i)) for i in both], axis=1)
            return dot_nt(ref[seg_at(start, size), :], rhs)

        def turned(ref, h, piece, x):
            o, start, size, kind = piece
            rows_h = slice(h * HDIM, (h + 1) * HDIM)
            if kind == 'pair':
                return jnp.concatenate(
                    [dot_nn(ref[rows_h, halves[i]], lanes(x, i)) for i in both], axis=1)
            return dot_nn(ref[rows_h, seg_at(start, size)], x)

        def add_rows(ref, piece, xs, stack):
            o, start, size, kind = piece
            if kind == 'pair':
                for i in both:
                    ref[halves[i], :] += dot_nn(
                        jnp.concatenate([lanes(x, i) for x in xs], axis=1),
                        jnp.concatenate([part(stack, i), part(stack, 2 + i)], axis=0))
            else:
                ref[seg_at(start, size), :] += dot_nn(jnp.concatenate(xs, axis=1), stack)

        def fold(x, op):
            return op(x.reshape(x.shape[0] // 8, 8, step), axis=0)

        tops = [[], []]
        sums = [[], []]
        for piece in pieces:
            o, start, size, kind = piece
            for h in both:
                s = left(kr, piece, qh[h])
                if kind == 'tri':
                    s = jnp.where(tri_mask, s, NEG)
                if kind == 'pair':
                    s = jnp.where(pair_mask, s, NEG)
                m = fold(s, jnp.max)
                top[h] = jnp.maximum(top[h], m)
                m = jnp.max(m, axis=0, keepdims=True)
                e = jnp.exp(s - m)
                s_ref[h, o:o + size, :] = e
                tops[h].append(m)
                sums[h].append(jnp.sum(fold(e, jnp.sum), axis=0, keepdims=True))
        scales = []
        for h in both:
            m = functools.reduce(jnp.maximum, tops[h])
            w = [jnp.exp(mc - m) for mc in tops[h]]
            inv = 1.0 / sum(wc * sc for wc, sc in zip(w, sums[h]))
            scales.append([wc * inv for wc in w])
        o_acc = [jnp.zeros((HDIM, step), f32)] * 2
        for n, piece in enumerate(pieces):
            o, start, size, kind = piece
            low = []
            for h in both:
                p = s_ref[h, o:o + size, :] * scales[h][n]
                s_ref[h, o:o + size, :] = p
                low.append(p.astype(bf16))
                o_acc[h] = o_acc[h] + turned(vt, h, piece, low[h])
            add_rows(dv, piece, low, d_stack)
        deltas = []
        for h in both:
            d_turned = jnp.concatenate(
                [dot_t[h * HDIM:(h + 1) * HDIM, halves[i]] for i in both], axis=1)
            deltas.append(jnp.sum(o_acc[h] * d_turned.astype(f32), axis=0, keepdims=True))
        dq_acc = [jnp.zeros((HDIM, step), f32)] * 2
        for n, piece in enumerate(pieces):
            o, start, size, kind = piece
            low = []
            for h in both:
                dp = left(vr, piece, dh[h])
                low.append((s_ref[h, o:o + size, :] * (dp - deltas[h])).astype(bf16))
                dq_acc[h] = dq_acc[h] + turned(kt, h, piece, low[h])
            add_rows(dk, piece, low, q_stack)
        o_rows = jnp.concatenate(o_acc, axis=0).T.astype(bf16)
        dq_rows = jnp.concatenate(dq_acc, axis=0).T
        for i in both:
            att[halves[i], :] = part(o_rows, i)
            dqn[halves[i], :] = part(dq_rows, i)

    for b in range(TRUNK // 2):
        block(b * step, b * step + SEG, [(c * step, step) for c in range(b)], True)
    trunk_chunks = [(c * step, step) for c in range(TRUNK // 2)]

    @pl.loop(0, BRANCHES // 2)
    def _(i):
        start = (TRUNK + 2 * i) * SEG
        block(start, start + SEG, trunk_chunks, False)

    @pl.loop(0, BRANCHES)
    def _(i):
        branch = TRUNK + i
        first = TREE_SEGS - 1
        last = TRUNK + BRANCHES
        for leaf in range(TREE_SEGS - 1, TRUNK + BRANCHES - 1, -1):
            first = jnp.where(par[leaf] == branch, leaf, first)
        for leaf in range(TRUNK + BRANCHES, TREE_SEGS):
            last = jnp.where(par[leaf] == branch, leaf, last)
        block(first * SEG, last * SEG, trunk_chunks + [(branch * SEG, SEG)], False)

    totals = [jnp.zeros((8, 2 * HDIM), f32)] * 3
    for i in range(size):
        here, there = places(i)
        cos, sin = cos_ref[there, :], sin_ref[there, :]
        att_ref[here, :] = att[there, :]
        dq = dqn[there, :] * (HDIM ** -0.5)
        dkr = dk[there, :]
        parts = [dq * cos - partner(dq) * sin, dkr * cos - partner(dkr) * sin, dv[there, :]]
        for c in range(3):
            low = parts[c].astype(bf16)
            g_ref[c, here, :] = low
            totals[c] = totals[c] + jnp.sum(low.astype(f32).reshape(local // 8, 8, 2 * HDIM), axis=0)

    rows_out = [jnp.sum(t, axis=0, keepdims=True) for t in totals]
    for h in range(2):
        rows_out.append(jnp.full((1, 2 * HDIM), jnp.max(top[h]), f32))
    rows_out.append(jnp.zeros((3, 2 * HDIM), f32))
    aux_ref[0] = jnp.concatenate(rows_out, axis=0)


def attention(parents, me, size, cos, sin, qkv, grad_att):
    rows, width = grad_att.shape
    pairs = width // (2 * HDIM)
    step = 2 * SEG
    wide = 2 * HDIM
    keys = TRUNK * SEG + 2 * SEG
    blk = lambda: pl.BlockSpec((rows, wide), lambda p, par, me: (0, p))
    blk3 = lambda: pl.BlockSpec((3, rows, wide), lambda p, par, me: (0, 0, p))
    tab = lambda: pl.BlockSpec((rows, wide), lambda p, par, me: (0, 0))
    return pl.pallas_call(
        functools.partial(attn_kernel, size),
        out_shape=(
            jax.ShapeDtypeStruct((rows, width), bf16),
            jax.ShapeDtypeStruct((3, rows, width), bf16),
            jax.ShapeDtypeStruct((pairs, 8, wide), f32),
        ),
        grid_spec=pltpu.PrefetchScalarGridSpec(
            num_scalar_prefetch=2,
            grid=(pairs,),
            in_specs=[tab(), tab(), blk3(), blk()],
            out_specs=[blk(), blk3(), pl.BlockSpec((1, 8, wide), lambda p, par, me: (p, 0, 0))],
            scratch_shapes=[
                pltpu.VMEM((rows, wide), bf16),
                pltpu.VMEM((rows, wide), bf16),
                pltpu.VMEM((rows, wide), bf16),
                pltpu.VMEM((rows, wide), bf16),
                pltpu.VMEM((wide, rows), bf16),
                pltpu.VMEM((wide, rows), bf16),
                pltpu.VMEM((wide, rows), bf16),
                pltpu.VMEM((rows, wide), bf16),
                pltpu.VMEM((rows, wide), f32),
                pltpu.VMEM((rows, wide), f32),
                pltpu.VMEM((rows, wide), f32),
                pltpu.VMEM((2, keys, step), f32),
                pltpu.VMEM((2, 8, step), f32),
            ],
        ),
        compiler_params=pltpu.CompilerParams(
            dimension_semantics=("arbitrary",), vmem_limit_bytes=40 << 20),
        cost_estimate=pl.CostEstimate(flops=60 * 10**9, transcendentals=17 * 10**6, bytes_accessed=24 << 20),
    )(parents, me, cos, sin, qkv, grad_att)


clip_tau = 10.0
norm_eps = 1e-05


def dot_tn(a, b):
    return lax.dot_general(a, b, (((0,), (0,)), ((), ())), preferred_element_type=f32)


def xor_send(x, bits, size):
    return lax.ppermute(x, "tensor", [(i, i ^ bits) for i in range(size)])


def gather_first(x, size):
    return [xor_send(x, i, size) for i in (range(1, size) if size != 4 else (1, 2))]


def gather_last(first, size):
    if size != 4:
        return first
    one, two = first
    half = one.shape[0] // 2
    low = xor_send(two[:half], 1, size)
    high = xor_send(one[half:], 2, size)
    return [one, two, low, high]


def add_low(a, b):
    return (a.astype(f32) + b.astype(f32)).astype(bf16)


def scatter_rest(parts, size):
    low, high = parts[0].astype(f32), parts[1].astype(f32)
    for i in range(1, size):
        low = low + xor_send(parts[2 * i], i, size).astype(f32)
        high = high + xor_send(parts[2 * i + 1], i, size).astype(f32)
    return [low, high]


def turn(values, *others):
    if not values:
        return values
    return list(lax.optimization_barrier(tuple(values) + others)[: len(values)])


def after(x, *others):
    return lax.optimization_barrier((x,) + others)[0]


class Carry:
    def __init__(self, sends, tag):
        self.sends, self.tag = sends, tag
        self.count = len(sends)
        self.specs = [pl.BlockSpec(memory_space=pl.ANY)] * self.count
        self.shapes = [jax.ShapeDtypeStruct(a.shape, a.dtype) for a, way in sends]
        self.arrays = [a for a, way in sends]
        self.scratch = [pltpu.SemaphoreType.DMA((2, self.count))] if sends else []

    def params(self, dims):
        extra = {"collective_id": self.tag, "has_side_effects": True} if self.sends else {}
        return pltpu.CompilerParams(
            dimension_semantics=("arbitrary",) * dims, vmem_limit_bytes=48 << 20, **extra)

    def run(self, grid, sources, targets, sems, compute):
        if not self.sends:
            compute()
            return
        at = [pl.program_id(n) for n in range(len(grid))]
        first, last = at[0] == 0, at[0] == grid[0] - 1
        for n in range(1, len(grid)):
            first, last = first & (at[n] == 0), last & (at[n] == grid[n] - 1)
        t = lax.axis_index("tensor")
        near = {1: t + 1 - 2 * (t % 2), 2: t + 2 - 4 * ((t // 2) % 2)}

        def copies():
            return [
                pltpu.make_async_remote_copy(
                    src_ref=sources[n],
                    dst_ref=targets[n],
                    send_sem=sems[0].at[0, n],
                    recv_sem=sems[0].at[1, n],
                    device_id={"tensor": near[way]},
                    device_id_type=pl.DeviceIdType.MESH,
                )
                for n, (a, way) in enumerate(self.sends)
            ]

        @pl.when(first)
        def _():
            barrier = pltpu.get_barrier_semaphore()
            for way in (1, 2):
                pl.semaphore_signal(
                    barrier, inc=1, device_id={"tensor": near[way]},
                    device_id_type=pl.DeviceIdType.MESH)
            pl.semaphore_wait(barrier, 2)
            for copy in copies():
                copy.start()

        compute()

        @pl.when(last)
        def _():
            for copy in copies():
                copy.wait()


def hint():
    return pl.CostEstimate(flops=10**10, transcendentals=0, bytes_accessed=2 << 20)


def chunk_matmul(pairs, columns, tile, count, starts, carry):
    x0 = pairs[0][0]
    local = x0.shape[-2] // count
    blocks = len(starts)
    x_specs, w_specs = [], []
    slope_of = (starts[-1] - starts[0]) // max(blocks - 1, 1)
    at = lambda i: starts[0] + slope_of * i
    for x, w, c in pairs:
        depth = x.shape[-1]
        if c is None or c < 0:
            x_specs.append(pl.BlockSpec((local, depth), lambda j, i: (at(i), 0)))
        else:
            x_specs.append(pl.BlockSpec((None, local, depth), lambda j, i, c=c: (c, at(i), 0)))
        if c is None:
            w_specs.append(pl.BlockSpec((depth, tile), lambda j, i: (0, j)))
        elif c < 0:
            w_specs.append(pl.BlockSpec((tile, depth), lambda j, i: (j, 0)))
        else:
            w_specs.append(pl.BlockSpec((None, tile, depth), lambda j, i, c=c: (c, j, 0)))
    terms = len(pairs)
    grid = (columns // tile, blocks)
    half = local // 2

    def kernel(*refs):
        ins = refs[: 2 * terms]
        sources = refs[2 * terms : 2 * terms + carry.count]
        outs = refs[2 * terms + carry.count :]
        targets, sems = outs[2 * blocks : 2 * blocks + carry.count], outs[2 * blocks + carry.count :]

        def compute():
            acc = None
            for n in range(terms):
                dot = dot_nn if pairs[n][2] is None else dot_nt
                term = dot(ins[n][...], ins[terms + n][...])
                acc = term if acc is None else acc + term
            low = acc.astype(bf16)
            for i in range(blocks):
                @pl.when(pl.program_id(1) == i)
                def _(i=i):
                    outs[2 * i][...] = low[:half]
                    outs[2 * i + 1][...] = low[half:]

        carry.run(grid, sources, targets, sems, compute)

    outs = pl.pallas_call(
        kernel,
        grid=grid,
        in_specs=x_specs + w_specs + carry.specs,
        out_specs=[pl.BlockSpec((half, tile), lambda j, i: (0, j))] * (2 * blocks) + carry.specs,
        out_shape=[jax.ShapeDtypeStruct((half, columns), bf16)] * (2 * blocks) + carry.shapes,
        scratch_shapes=carry.scratch,
        compiler_params=carry.params(2),
        cost_estimate=hint(),
    )(*[p[0] for p in pairs], *[p[1] for p in pairs], *carry.arrays)
    pieces = {}
    for n, b in enumerate(starts):
        pieces[2 * b], pieces[2 * b + 1] = outs[2 * n], outs[2 * n + 1]
    return pieces, list(outs[2 * blocks :])


def weight_grad(x, y, m_tile, n_tile, carry):
    rows, m = x.shape
    n = y.shape[-1]
    if y.ndim == 3:
        grid = (y.shape[0], m // m_tile, n // n_tile)
        y_spec = pl.BlockSpec((None, rows, n_tile), lambda c, i, j: (c, 0, j))
        o_spec = pl.BlockSpec((None, m_tile, n_tile), lambda c, i, j: (c, i, j))
        shape = (y.shape[0], m, n)
    else:
        grid = (1, m // m_tile, n // n_tile)
        y_spec = pl.BlockSpec((rows, n_tile), lambda c, i, j: (0, j))
        o_spec = pl.BlockSpec((m_tile, n_tile), lambda c, i, j: (i, j))
        shape = (m, n)

    def kernel(x_ref, y_ref, *refs):
        sources, (o_ref, *rest) = refs[: carry.count], refs[carry.count :]
        targets, sems = rest[: carry.count], rest[carry.count :]

        def compute():
            o_ref[...] = dot_tn(x_ref[...], y_ref[...]).astype(bf16)

        carry.run(grid, sources, targets, sems, compute)

    outs = pl.pallas_call(
        kernel,
        grid=grid,
        in_specs=[pl.BlockSpec((rows, m_tile), lambda c, i, j: (0, i)), y_spec] + carry.specs,
        out_specs=[o_spec] + carry.specs,
        out_shape=[jax.ShapeDtypeStruct(shape, bf16)] + carry.shapes,
        scratch_shapes=carry.scratch,
        compiler_params=carry.params(3),
        cost_estimate=hint(),
    )(x, y, *carry.arrays)
    return outs[0], list(outs[1:])


def hidden_grad(cot, down_w, slope, r_tile, f_tile, carry):
    rows, model = cot.shape
    ff = down_w.shape[0]
    grid = (ff // f_tile, rows // r_tile)

    def kernel(c_ref, w_ref, s_ref, *refs):
        sources, (g_ref, b_ref, *rest) = refs[: carry.count], refs[carry.count :]
        targets, sems = rest[: carry.count], rest[carry.count :]

        def compute():
            low = (dot_nt(c_ref[...], w_ref[...]) * s_ref[...].astype(f32)).astype(bf16)
            g_ref[...] = low
            part = jnp.sum(low.astype(f32).reshape(r_tile // 8, 8, f_tile), axis=0)

            @pl.when(pl.program_id(1) == 0)
            def _():
                b_ref[...] = part

            @pl.when(pl.program_id(1) > 0)
            def _():
                b_ref[...] += part

        carry.run(grid, sources, targets, sems, compute)

    outs = pl.pallas_call(
        kernel,
        grid=grid,
        in_specs=[
            pl.BlockSpec((r_tile, model), lambda j, i: (i, 0)),
            pl.BlockSpec((f_tile, model), lambda j, i: (j, 0)),
            pl.BlockSpec((r_tile, f_tile), lambda j, i: (i, j)),
        ] + carry.specs,
        out_specs=[
            pl.BlockSpec((r_tile, f_tile), lambda j, i: (i, j)),
            pl.BlockSpec((8, f_tile), lambda j, i: (0, j)),
        ] + carry.specs,
        out_shape=[
            jax.ShapeDtypeStruct((rows, ff), bf16),
            jax.ShapeDtypeStruct((8, ff), f32),
        ] + carry.shapes,
        scratch_shapes=carry.scratch,
        compiler_params=carry.params(2),
        cost_estimate=hint(),
    )(cot, down_w, slope, *carry.arrays)
    return outs[0], jnp.sum(outs[1], axis=0), list(outs[2:])


def dp_totals(sums, tops, groups, start):
    step = 1
    sums, tops = turn([sums, tops], start)
    while step < groups:
        way = [(i, i ^ step) for i in range(groups)]
        both = jnp.concatenate([sums, jnp.zeros((1, 128), f32).at[0, : tops.shape[0]].set(tops)], axis=0)
        other = lax.ppermute(both, "dp", way)
        sums = sums + other[:-1]
        tops = jnp.maximum(tops, other[-1, : tops.shape[0]])
        step *= 2
    return sums, tops


def norm_parts(rows_in):
    row_mean = jnp.mean(rows_in, axis=-1, keepdims=True)
    centred = rows_in - row_mean
    inverse = lax.rsqrt(jnp.mean(centred * centred, axis=-1, keepdims=True) + norm_eps)
    return centred * inverse, inverse


def gelu_parts(v):
    scale = (2.0 / jnp.pi) ** 0.5
    square = v * v
    t = jnp.tanh(scale * (v + 0.044715 * v * square))
    half = 0.5 * (1.0 + t)
    slope = half + 0.5 * v * (1.0 - t * t) * (scale * (1.0 + (3 * 0.044715) * square))
    return v * half, slope


def body(
    tokens,
    cotangent,
    ln_gain,
    ln_bias,
    w_qkv,
    b_qkv,
    w_out,
    w_fc1,
    b_fc1,
    w_fc2,
    resid_bias,
    parents,
):
    size = lax.axis_size("tensor")
    groups = lax.axis_size("dp")
    local_rows, model = tokens.shape
    total_rows = local_rows * size
    me = lax.axis_index("tensor")
    width = w_qkv.shape[2]
    heads = width // HDIM

    cos, sin = rope_tables()
    tokens_f = tokens.astype(f32)
    xhat, inverse = norm_parts(tokens_f)
    normed_local = (xhat * ln_gain + ln_bias).astype(bf16)
    up_w = lax.all_gather(w_fc1, "dp", axis=0, tiled=True)
    qkv_w = lax.all_gather(w_qkv, "dp", axis=1, tiled=True)
    out_w = lax.all_gather(w_out, "dp", axis=1, tiled=True)
    down_w = lax.all_gather(w_fc2, "dp", axis=1, tiled=True)
    normed_first = gather_first(normed_local, size)
    normed_parts = gather_last(normed_first, size)
    normed = jnp.concatenate([normed_local] + normed_parts, axis=0)
    cot_first = gather_first(after(cotangent, normed_first[0]), size)
    normed, cos, sin = lax.optimization_barrier((normed, cos, sin))

    hidden_pre = dot_nn(normed, up_w) + b_fc1
    activated, slope = gelu_parts(hidden_pre)
    activated, slope = lax.optimization_barrier((activated.astype(bf16), slope.astype(bf16)))
    cot_first = turn(cot_first, activated)
    cot_parts = gather_last(cot_first, size)
    projected = (
        jnp.einsum("td,cdh->cth", after(normed, activated, *cot_first), qkv_w, preferred_element_type=f32)
        + b_qkv[:, None, :]
    ).astype(bf16)
    cot_parts = turn(cot_parts, projected)
    cot_full = jnp.concatenate([cotangent] + cot_parts, axis=0)
    grad_w_fc2 = dot_tn(activated, cot_full).astype(bf16)
    summed_fc2 = lax.psum_scatter(grad_w_fc2, "dp", scatter_dimension=1, tiled=True)
    grad_attended = dot_nt(after(cot_full, grad_w_fc2), out_w).astype(bf16)
    attended, grad_qkv, aux = attention(
        parents[0], me[None], size, cos, sin, projected, grad_attended)
    grad_b_qkv = jnp.transpose(aux[:, :3], (1, 0, 2)).reshape(-1)
    tops = aux[:, 3:5, 0].reshape(-1)

    four = size == 4
    none = lambda: Carry([], 0)
    backs = [(grad_qkv, qkv_w, c) for c in range(3)]
    everyone = tuple(range(size - 1, -1, -1))
    far, near = everyone[0::2], everyone[1::2]
    half_rows = model // 2
    grad_w_out = dot_tn(attended, cot_full).astype(bf16)
    summed_out = lax.psum_scatter(grad_w_out, "dp", scatter_dimension=1, tiled=True)
    branch, ignored = chunk_matmul(
        [(after(attended, grad_w_out), out_w, None), (activated, down_w, None)],
        model, half_rows, size, everyone, none())
    grad_w_qkv, got = weight_grad(
        after(normed, branch[0]), grad_qkv, half_rows, width,
        Carry([(branch[6], 1), (branch[7], 2)], 0) if four else none())
    summed_qkv = lax.psum_scatter(grad_w_qkv, "dp", scatter_dimension=1, tiled=True)
    branch_next = [add_low(branch[3], got[1]), add_low(branch[4], got[0])] if four else []
    grad_hidden, grad_b_fc1, got = hidden_grad(
        after(cot_full, grad_w_qkv, *branch_next), down_w, slope, local_rows, half_rows,
        Carry([(branch[2], 1), (branch[5], 2)], 1) if four else none())
    sums = jnp.concatenate([grad_b_qkv, grad_b_fc1]).reshape(-1, 128)
    normed_part, more = chunk_matmul(
        backs + [(after(grad_hidden, summed_fc2), up_w, -1)], model, half_rows, size, far,
        Carry([(branch_next[0], 1), (branch_next[1], 2)], 2) if four else none())
    sums, tops = dp_totals(sums, tops, groups, normed_part[2 * far[0]])
    if four:
        branch_sum = [
            branch[0].astype(f32) + got[0].astype(f32) + more[1].astype(f32),
            branch[1].astype(f32) + more[0].astype(f32) + got[1].astype(f32)]
    else:
        branch_sum = scatter_rest(branch, size)
    output_rows = (tokens_f + jnp.concatenate(branch_sum, axis=0) + resid_bias).astype(bf16)
    grad_w_fc1, got = weight_grad(
        after(normed, normed_part[2 * far[0]], summed_out), grad_hidden, half_rows, half_rows,
        Carry([(normed_part[6], 1), (normed_part[7], 2)], 3) if four else none())
    summed_fc1 = lax.psum_scatter(grad_w_fc1, "dp", scatter_dimension=0, tiled=True)
    late, more = chunk_matmul(
        backs + [(after(grad_hidden, grad_w_fc1, output_rows), up_w, -1)],
        model, half_rows, size, near,
        Carry([(normed_part[2], 1)], 4) if four else none())
    normed_part |= late
    if four:
        one = xor_send(add_low(normed_part[3], got[1]), 1, size).astype(f32)
        two = xor_send(add_low(normed_part[4], got[0]), 2, size).astype(f32)
        side = xor_send(normed_part[5], 2, size).astype(f32)
        grad_normed = [
            normed_part[0].astype(f32) + more[0].astype(f32) + two,
            normed_part[1].astype(f32) + one + side]
    else:
        grad_normed = scatter_rest(normed_part, size)
    grad_normed = jnp.concatenate(grad_normed, axis=0)
    summed_fc1, summed_out, summed_qkv, summed_fc2 = (
        w.astype(f32) for w in (summed_fc1, summed_out, summed_qkv, summed_fc2))

    sums = sums.reshape(-1)
    bias_qkv = sums[: 3 * width].reshape(3, width)
    bias_fc1 = sums[3 * width :]
    head_top = tops
    factor = jnp.sqrt(clip_tau / jnp.maximum(head_top, clip_tau))
    clipped_qk = (w_qkv[:2].astype(f32) * jnp.repeat(factor, HDIM)[None, None, :]).astype(bf16)

    grad_xhat = grad_normed * ln_gain
    cot_local = cotangent.astype(f32)
    input_grad = cot_local + inverse * (
        grad_xhat
        - jnp.mean(grad_xhat, axis=-1, keepdims=True)
        - xhat * jnp.mean(grad_xhat * xhat, axis=-1, keepdims=True)
    )
    terms = jnp.stack(
        [jnp.sum(grad_normed * xhat, axis=0), jnp.sum(grad_normed, axis=0), jnp.sum(cot_local, axis=0)]
    )
    every = size * groups
    pieces = jnp.transpose(terms.reshape(3, every, model // every), (1, 0, 2)).reshape(every, -1)
    pieces = lax.all_to_all(pieces, ("dp", "tensor"), 0, 0, tiled=True)
    grad_small = jnp.sum(pieces, axis=0).reshape(3, model // every)
    return (
        output_rows,
        input_grad,
        grad_small,
        summed_qkv,
        bias_qkv,
        summed_out,
        summed_fc1,
        bias_fc1,
        summed_fc2,
        clipped_qk,
    )


def solution(mesh):
    return jax.shard_map(
        body,
        mesh=mesh,
        in_specs=(
            P(("dp", "tensor"), None),
            P(("dp", "tensor"), None),
            P(),
            P(),
            P(None, "dp", "tensor"),
            P(None, "tensor"),
            P("tensor", "dp"),
            P("dp", "tensor"),
            P("tensor"),
            P("tensor", "dp"),
            P(),
            P("dp", None),
        ),
        out_specs=(
            P(("dp", "tensor"), None),
            P(("dp", "tensor"), None),
            P(None, ("dp", "tensor")),
            P(None, "dp", "tensor"),
            P(None, "tensor"),
            P("tensor", "dp"),
            P("dp", "tensor"),
            P("tensor"),
            P("tensor", "dp"),
            P(None, "dp", "tensor"),
        ),
        check_vma=False,
    )
```

```python
import functools

import jax
import jax.numpy as jnp
import numpy as np
from jax import lax
from jax.experimental import pallas as pl
from jax.experimental.pallas import tpu as pltpu
from jax.sharding import PartitionSpec as P

HDIM = 64
ROT = 32
SEG = 128
TRUNK = 6
BRANCHES = 4
LEAVES = 2
TREE_SEGS = TRUNK + BRANCHES + BRANCHES * LEAVES
bf16 = jnp.bfloat16
f32 = jnp.float32
NEG = -1e30
rope_base = 10000.0


def dot_nn(a, b):
    return lax.dot_general(a, b, (((1,), (0,)), ((), ())), preferred_element_type=f32)


def dot_nt(a, b):
    return lax.dot_general(a, b, (((1,), (1,)), ((), ())), preferred_element_type=f32)


def rope_tables():
    lane = np.arange(2 * HDIM) % HDIM
    freq = np.where(lane < ROT, rope_base ** (-2.0 * (lane % (ROT // 2)) / ROT), 0.0)
    angles = np.concatenate([np.arange(SEG), SEG * np.arange(TRUNK + 2)])[:, None] * freq[None, :]
    return np.cos(angles).astype(np.float32), np.sin(angles).astype(np.float32)


def partner(x):
    lane = lax.broadcasted_iota(jnp.int32, x.shape, 1) % HDIM
    half = ROT // 2
    return jnp.where(lane < half, pltpu.roll(x, 2 * HDIM - half, 1), pltpu.roll(x, half, 1))


def attn_kernel(size, par, me, cos_in, sin_in, qkv_ref, do_in, att_ref, g_ref, aux_ref,
                qs, kr, vr, do_ref, kt, vt, dot_t, att, dqn, dk, dv, s_ref, top, cos_ref, sin_ref):
    rows = TREE_SEGS * SEG
    step = 2 * SEG
    local = rows // size
    lane_low = lax.broadcasted_iota(jnp.int32, (step, 2 * HDIM), 1) < HDIM

    def unit(n):
        return jnp.where(
            lax.broadcasted_iota(jnp.int32, (n, n), 0) == lax.broadcasted_iota(jnp.int32, (n, n), 1),
            1.0, 0.0).astype(bf16)

    unit_wide = unit(2 * HDIM)

    def places(i):
        here = pl.ds(i * local, local)
        there = pl.ds(pl.multiple_of((me[0] ^ i) * local, local), local)
        return here, there

    @pl.when(pl.program_id(0) == 0)
    def _():
        sign = jnp.where(lax.broadcasted_iota(jnp.int32, (SEG, 2 * HDIM), 1) % HDIM < ROT // 2, -1.0, 1.0)
        cos_place, sin_place = cos_in[:SEG, :], sin_in[:SEG, :]
        for depth in range(TRUNK + 2):
            cos_seg, sin_seg = cos_in[SEG + depth : SEG + depth + 1, :], sin_in[SEG + depth : SEG + depth + 1, :]
            cos = cos_place * cos_seg - sin_place * sin_seg
            sin = (sin_place * cos_seg + cos_place * sin_seg) * sign
            first = [depth] if depth < TRUNK else range(TRUNK, TRUNK + BRANCHES)
            for seg in first if depth <= TRUNK else range(TRUNK + BRANCHES, TREE_SEGS):
                cos_ref[seg * SEG : (seg + 1) * SEG, :] = cos
                sin_ref[seg * SEG : (seg + 1) * SEG, :] = sin

    for i in range(size):
        here, there = places(i)
        cos, sin = cos_ref[there, :], sin_ref[there, :]
        q = qkv_ref[0, here, :].astype(f32)
        k = qkv_ref[1, here, :].astype(f32)
        qs[there, :] = ((q * cos + partner(q) * sin) * (HDIM ** -0.5)).astype(bf16)
        kr[there, :] = (k * cos + partner(k) * sin).astype(bf16)
        vr[there, :] = qkv_ref[2, here, :]
        do_ref[there, :] = do_in[here, :]

    for i in range(rows // step):
        at = pl.ds(i * step, step)
        kt[:, at] = dot_nt(unit_wide, kr[at, :]).astype(bf16)
        vt[:, at] = dot_nt(unit_wide, vr[at, :]).astype(bf16)
        dot_t[:, at] = dot_nt(unit_wide, do_ref[at, :]).astype(bf16)
        dk[at, :] = jnp.zeros((step, 2 * HDIM), f32)
        dv[at, :] = jnp.zeros((step, 2 * HDIM), f32)

    top[...] = jnp.full((2, 8, step), NEG, f32)
    key_id = lax.broadcasted_iota(jnp.int32, (SEG, step), 0)
    query_id = lax.broadcasted_iota(jnp.int32, (SEG, step), 1) % SEG
    pair_mask = key_id <= query_id
    tri_mask = lax.broadcasted_iota(jnp.int32, (step, step), 0) <= lax.broadcasted_iota(
        jnp.int32, (step, step), 1)

    def seg_at(start, size):
        if isinstance(start, int):
            return pl.ds(start, size)
        return pl.ds(pl.multiple_of(start, SEG), size)

    def block(q0, q1, chunks, diag):
        halves = [seg_at(q0, SEG), seg_at(q1, SEG)]
        q_all = jnp.concatenate([qs[halves[0], :], qs[halves[1], :]], axis=0)
        do_all = jnp.concatenate([do_ref[halves[0], :], do_ref[halves[1], :]], axis=0)
        zero = jnp.zeros_like(q_all)
        pieces = []
        off = 0
        for start, size in chunks:
            pieces.append((off, start, size, 'full'))
            off += size
        pieces.append((off, q0, step, 'tri') if diag else (off, None, SEG, 'pair'))
        both = range(2)
        qh = [jnp.where(lane_low if h == 0 else ~lane_low, q_all, zero) for h in both]
        dh = [jnp.where(lane_low if h == 0 else ~lane_low, do_all, zero) for h in both]
        q_stack = jnp.concatenate(qh, axis=0)
        d_stack = jnp.concatenate(dh, axis=0)

        def part(x, i):
            return x[i * SEG:(i + 1) * SEG]

        def lanes(x, i):
            return x[:, i * SEG:(i + 1) * SEG]

        def left(ref, piece, rhs):
            o, start, size, kind = piece
            if kind == 'pair':
                return jnp.concatenate(
                    [dot_nt(ref[halves[i], :], part(rhs, i)) for i in both], axis=1)
            return dot_nt(ref[seg_at(start, size), :], rhs)

        def turned(ref, h, piece, x):
            o, start, size, kind = piece
            rows_h = slice(h * HDIM, (h + 1) * HDIM)
            if kind == 'pair':
                return jnp.concatenate(
                    [dot_nn(ref[rows_h, halves[i]], lanes(x, i)) for i in both], axis=1)
            return dot_nn(ref[rows_h, seg_at(start, size)], x)

        def add_rows(ref, piece, xs, stack):
            o, start, size, kind = piece
            if kind == 'pair':
                for i in both:
                    ref[halves[i], :] += dot_nn(
                        jnp.concatenate([lanes(x, i) for x in xs], axis=1),
                        jnp.concatenate([part(stack, i), part(stack, 2 + i)], axis=0))
            else:
                ref[seg_at(start, size), :] += dot_nn(jnp.concatenate(xs, axis=1), stack)

        def fold(x, op):
            return op(x.reshape(x.shape[0] // 8, 8, step), axis=0)

        tops = [[], []]
        sums = [[], []]
        for piece in pieces:
            o, start, size, kind = piece
            for h in both:
                s = left(kr, piece, qh[h])
                if kind == 'tri':
                    s = jnp.where(tri_mask, s, NEG)
                if kind == 'pair':
                    s = jnp.where(pair_mask, s, NEG)
                m = fold(s, jnp.max)
                top[h] = jnp.maximum(top[h], m)
                m = jnp.max(m, axis=0, keepdims=True)
                e = jnp.exp(s - m)
                s_ref[h, o:o + size, :] = e
                tops[h].append(m)
                sums[h].append(jnp.sum(fold(e, jnp.sum), axis=0, keepdims=True))
        scales = []
        for h in both:
            m = functools.reduce(jnp.maximum, tops[h])
            w = [jnp.exp(mc - m) for mc in tops[h]]
            inv = 1.0 / sum(wc * sc for wc, sc in zip(w, sums[h]))
            scales.append([wc * inv for wc in w])
        o_acc = [jnp.zeros((HDIM, step), f32)] * 2
        for n, piece in enumerate(pieces):
            o, start, size, kind = piece
            low = []
            for h in both:
                p = s_ref[h, o:o + size, :] * scales[h][n]
                s_ref[h, o:o + size, :] = p
                low.append(p.astype(bf16))
                o_acc[h] = o_acc[h] + turned(vt, h, piece, low[h])
            add_rows(dv, piece, low, d_stack)
        deltas = []
        for h in both:
            d_turned = jnp.concatenate(
                [dot_t[h * HDIM:(h + 1) * HDIM, halves[i]] for i in both], axis=1)
            deltas.append(jnp.sum(o_acc[h] * d_turned.astype(f32), axis=0, keepdims=True))
        dq_acc = [jnp.zeros((HDIM, step), f32)] * 2
        for n, piece in enumerate(pieces):
            o, start, size, kind = piece
            low = []
            for h in both:
                dp = left(vr, piece, dh[h])
                low.append((s_ref[h, o:o + size, :] * (dp - deltas[h])).astype(bf16))
                dq_acc[h] = dq_acc[h] + turned(kt, h, piece, low[h])
            add_rows(dk, piece, low, q_stack)
        o_rows = jnp.concatenate(o_acc, axis=0).T.astype(bf16)
        dq_rows = jnp.concatenate(dq_acc, axis=0).T
        for i in both:
            att[halves[i], :] = part(o_rows, i)
            dqn[halves[i], :] = part(dq_rows, i)

    for b in range(TRUNK // 2):
        block(b * step, b * step + SEG, [(c * step, step) for c in range(b)], True)
    trunk_chunks = [(c * step, step) for c in range(TRUNK // 2)]

    @pl.loop(0, BRANCHES // 2)
    def _(i):
        start = (TRUNK + 2 * i) * SEG
        block(start, start + SEG, trunk_chunks, False)

    @pl.loop(0, BRANCHES)
    def _(i):
        branch = TRUNK + i
        first = TREE_SEGS - 1
        last = TRUNK + BRANCHES
        for leaf in range(TREE_SEGS - 1, TRUNK + BRANCHES - 1, -1):
            first = jnp.where(par[leaf] == branch, leaf, first)
        for leaf in range(TRUNK + BRANCHES, TREE_SEGS):
            last = jnp.where(par[leaf] == branch, leaf, last)
        block(first * SEG, last * SEG, trunk_chunks + [(branch * SEG, SEG)], False)

    totals = [jnp.zeros((8, 2 * HDIM), f32)] * 3
    for i in range(size):
        here, there = places(i)
        cos, sin = cos_ref[there, :], sin_ref[there, :]
        att_ref[here, :] = att[there, :]
        dq = dqn[there, :] * (HDIM ** -0.5)
        dkr = dk[there, :]
        parts = [dq * cos - partner(dq) * sin, dkr * cos - partner(dkr) * sin, dv[there, :]]
        for c in range(3):
            low = parts[c].astype(bf16)
            g_ref[c, here, :] = low
            totals[c] = totals[c] + jnp.sum(low.astype(f32).reshape(local // 8, 8, 2 * HDIM), axis=0)

    rows_out = [jnp.sum(t, axis=0, keepdims=True) for t in totals]
    for h in range(2):
        rows_out.append(jnp.full((1, 2 * HDIM), jnp.max(top[h]), f32))
    rows_out.append(jnp.zeros((3, 2 * HDIM), f32))
    aux_ref[0] = jnp.concatenate(rows_out, axis=0)


def attention(parents, me, size, cos, sin, qkv, grad_att):
    rows, width = grad_att.shape
    pairs = width // (2 * HDIM)
    step = 2 * SEG
    wide = 2 * HDIM
    keys = TRUNK * SEG + 2 * SEG
    blk = lambda: pl.BlockSpec((rows, wide), lambda p, par, me: (0, p))
    blk3 = lambda: pl.BlockSpec((3, rows, wide), lambda p, par, me: (0, 0, p))
    tab = lambda: pl.BlockSpec((SEG + TRUNK + 2, wide), lambda p, par, me: (0, 0))
    return pl.pallas_call(
        functools.partial(attn_kernel, size),
        out_shape=(
            jax.ShapeDtypeStruct((rows, width), bf16),
            jax.ShapeDtypeStruct((3, rows, width), bf16),
            jax.ShapeDtypeStruct((pairs, 8, wide), f32),
        ),
        grid_spec=pltpu.PrefetchScalarGridSpec(
            num_scalar_prefetch=2,
            grid=(pairs,),
            in_specs=[tab(), tab(), blk3(), blk()],
            out_specs=[blk(), blk3(), pl.BlockSpec((1, 8, wide), lambda p, par, me: (p, 0, 0))],
            scratch_shapes=[
                pltpu.VMEM((rows, wide), bf16),
                pltpu.VMEM((rows, wide), bf16),
                pltpu.VMEM((rows, wide), bf16),
                pltpu.VMEM((rows, wide), bf16),
                pltpu.VMEM((wide, rows), bf16),
                pltpu.VMEM((wide, rows), bf16),
                pltpu.VMEM((wide, rows), bf16),
                pltpu.VMEM((rows, wide), bf16),
                pltpu.VMEM((rows, wide), f32),
                pltpu.VMEM((rows, wide), f32),
                pltpu.VMEM((rows, wide), f32),
                pltpu.VMEM((2, keys, step), f32),
                pltpu.VMEM((2, 8, step), f32),
                pltpu.VMEM((rows, wide), f32),
                pltpu.VMEM((rows, wide), f32),
            ],
        ),
        compiler_params=pltpu.CompilerParams(
            dimension_semantics=("arbitrary",), vmem_limit_bytes=63 << 20),
        cost_estimate=pl.CostEstimate(flops=60 * 10**9, transcendentals=17 * 10**6, bytes_accessed=24 << 20),
    )(parents, me, cos, sin, qkv, grad_att)


clip_tau = 10.0
norm_eps = 1e-05


def dot_tn(a, b):
    return lax.dot_general(a, b, (((0,), (0,)), ((), ())), preferred_element_type=f32)


def xor_send(x, bits, size):
    return lax.ppermute(x, "tensor", [(i, i ^ bits) for i in range(size)])


def add_low(a, b):
    return (a.astype(f32) + b.astype(f32)).astype(bf16)


def scatter_rest(parts, size):
    low, high = parts[0].astype(f32), parts[1].astype(f32)
    for i in range(1, size):
        low = low + xor_send(parts[2 * i], i, size).astype(f32)
        high = high + xor_send(parts[2 * i + 1], i, size).astype(f32)
    return [low, high]


def after(x, *others):
    return lax.optimization_barrier((x,) + others)[0]


class Carry:
    def __init__(self, tag=0, arrays=(), shapes=(), links=None, count=0, alias=False):
        self.tag, self.arrays, self.links, self.count, self.alias = tag, list(arrays), links, count, alias
        self.shapes = [jax.ShapeDtypeStruct(*shape) for shape in shapes]


def sending(tag, *sends):
    return Carry(
        tag, [a for a, axis, bits in sends], [(a.shape, a.dtype) for a, axis, bits in sends],
        lambda src, dst: [(src[n], dst[n], axis, bits) for n, (a, axis, bits) in enumerate(sends)], len(sends))


def other_device(axis, bits):
    t = lax.axis_index(axis)
    at = t
    for n in range(8):
        if bits >> n & 1:
            at = at + (1 << n) - (2 << n) * ((t // (1 << n)) % 2)
    return {axis: at}


def meet(partners):
    barrier = pltpu.get_barrier_semaphore()
    for axis, bits in partners:
        pl.semaphore_signal(
            barrier, inc=1, device_id=other_device(axis, bits), device_id_type=pl.DeviceIdType.MESH)
    pl.semaphore_wait(barrier, len(partners))


def remote_copies(links, sems):
    return [
        pltpu.make_async_copy(src, dst, sems.at[0, n])
        if axis is None
        else pltpu.make_async_remote_copy(
            src_ref=src,
            dst_ref=dst,
            send_sem=sems.at[0, n],
            recv_sem=sems.at[1, n],
            device_id=other_device(axis, bits),
            device_id_type=pl.DeviceIdType.MESH,
        )
        for n, (src, dst, axis, bits) in enumerate(links)
    ]


def hint():
    return pl.CostEstimate(flops=10**10, transcendentals=0, bytes_accessed=2 << 20)


def tiled(inner, grid, ins, outs, carry=None, vmem=63):
    carry = carry or Carry()
    n_in, n_out, n_src, n_dst = len(ins), len(outs), len(carry.arrays), len(carry.shapes)
    in_specs = [pl.BlockSpec(block, at) for a, block, at in ins]
    out_specs = [pl.BlockSpec(block, at) for shape, dtype, block, at in outs]
    any_spec = pl.BlockSpec(memory_space=pltpu.HBM)
    arrays = [a for a, block, at in ins]
    shapes = [jax.ShapeDtypeStruct(shape, dtype) for shape, dtype, block, at in outs]
    if not carry.count:
        results = pl.pallas_call(
            inner, grid=grid, in_specs=in_specs, out_specs=out_specs, out_shape=shapes,
            compiler_params=pltpu.CompilerParams(
                dimension_semantics=("arbitrary",) * len(grid), vmem_limit_bytes=vmem << 20),
            cost_estimate=hint(),
        )(*arrays)
        return list(results), []

    def kernel(*refs):
        sources = refs[n_in : n_in + n_src]
        places = refs[n_in + n_src : n_in + n_src + n_out]
        targets = refs[n_in + n_src + n_out : -1]
        links = carry.links(sources, targets)
        meet(sorted(set((axis, bits) for src, dst, axis, bits in links if axis is not None)))
        copies = remote_copies(links, refs[-1])
        for copy in copies:
            copy.start()
        if grid:
            pltpu.emit_pipeline(inner, grid=grid, in_specs=in_specs, out_specs=out_specs)(*refs[:n_in], *places)
        for copy in copies:
            copy.wait()

    results = pl.pallas_call(
        kernel,
        in_specs=[any_spec] * (n_in + n_src),
        out_specs=[any_spec] * (n_out + n_dst),
        out_shape=shapes + carry.shapes,
        scratch_shapes=[pltpu.SemaphoreType.DMA((2, carry.count))],
        input_output_aliases={n_in: n_out} if carry.alias else {},
        compiler_params=pltpu.CompilerParams(
            vmem_limit_bytes=vmem << 20, collective_id=carry.tag, has_side_effects=True),
        cost_estimate=hint(),
    )(*arrays, *carry.arrays)
    return list(results[:n_out]), list(results[n_out:])


def side_sums(adds, grid):
    at = lambda j, i: (0, j * grid[1] + i)
    block = lambda a: (a.shape[0], a.shape[1] // (grid[0] * grid[1]))
    ins = [(a, block(a), at) for pair in adds for a in pair]
    outs = [(a.shape, a.dtype, block(a), at) for a, b in adds]
    return ins, outs


def chunk_matmul(pairs, columns, tile, count, blocks, at, carry=None, adds=(), cut=1):
    local = pairs[0][0].shape[-2] // count
    grid = (columns // tile, blocks)
    ins = []
    for x, w, c, d in pairs:
        depth = x.shape[-1]
        if c < 0:
            ins.append((x, (local, depth), lambda j, i: (at(i), 0)))
        else:
            ins.append((x, (None, local, depth), lambda j, i, c=c: (c, at(i), 0)))
        if d is None:
            ins.append((w, (depth, tile), lambda j, i: (0, j)))
        elif d < 0:
            ins.append((w, (tile, depth), lambda j, i: (j, 0)))
        else:
            ins.append((w, (None, tile, depth), lambda j, i, d=d: (d, j, 0)))
    terms = len(pairs)
    adds = dict(adds)
    more = [(adds[b], (local, tile), lambda j, i: (0, j)) for b in sorted(adds)]
    part = local // cut
    outs = [((part, columns), bf16, (part, tile), lambda j, i: (0, j))] * (blocks * cut)

    def inner(*refs):
        sides, results = dict(zip(sorted(adds), refs[2 * terms :])), refs[2 * terms + len(more) :]
        acc = None
        for n in range(terms):
            dot = dot_nn if pairs[n][3] is None else dot_nt
            term = dot(refs[2 * n][...], refs[2 * n + 1][...])
            acc = term if acc is None else acc + term
        for i in range(blocks):
            @pl.when(pl.program_id(1) == i)
            def _(i=i):
                whole = acc
                if at(i) in sides:
                    whole = whole + sides[at(i)][...].astype(f32)
                low = whole.astype(bf16)
                for n in range(cut):
                    results[i * cut + n][...] = low[n * part : (n + 1) * part]

    results, got = tiled(inner, grid, ins + more, outs, carry)
    return {at(i) * cut + n: results[i * cut + n] for i in range(blocks) for n in range(cut)}, got


def head_grads(normed, grad_qkv, cot, attended, tile, carry):
    rows, model = normed.shape
    width = attended.shape[1]
    last = model // tile - 1

    def inner(n_ref, g_ref, c_ref, a_ref, o_ref):
        @pl.when(pl.program_id(0) < 3)
        def _():
            o_ref[...] = dot_tn(n_ref[...], g_ref[...]).astype(bf16)

        @pl.when(pl.program_id(0) == 3)
        def _():
            o_ref[...] = dot_tn(c_ref[...], a_ref[...]).astype(bf16)

    (grads,), got = tiled(
        inner, (4, model // tile),
        [
            (normed, (rows, tile), lambda c, i: (0, i + (last - i) * (c // 3))),
            (grad_qkv, (None, rows, width), lambda c, i: (c - c // 3, 0, 0)),
            (cot, (rows, tile), lambda c, i: (0, i * (c // 3))),
            (attended, (rows, width), lambda c, i: (0, 0)),
        ],
        [((4, model, width), bf16, (None, tile, width), lambda c, i: (c, i, 0))], carry)
    return grads, got


def weight_grad(x, y, m_tile, n_tile, carry):
    rows, m = x.shape
    n = y.shape[1]

    def inner(x_ref, y_ref, o_ref):
        o_ref[...] = dot_tn(x_ref[...], y_ref[...]).astype(bf16)

    (grad,), got = tiled(
        inner, (m // m_tile, n // n_tile),
        [(x, (rows, m_tile), lambda i, j: (0, i)), (y, (rows, n_tile), lambda i, j: (0, j))],
        [((m, n), bf16, (m_tile, n_tile), lambda i, j: (i, j))], carry)
    return grad, got


def hidden_forward(normed, up_w, b_fc1, r_tile, f_tile, carry):
    rows, model = normed.shape
    ff = up_w.shape[1]

    def inner(n_ref, w_ref, b_ref, a_ref, s_ref):
        value, slope = gelu_parts(dot_nn(n_ref[...], w_ref[...]) + b_ref[...])
        a_ref[...] = value.astype(bf16)
        s_ref[...] = slope.astype(bf16)

    out = ((rows, ff), bf16, (r_tile, f_tile), lambda j, i: (i, j))
    (value, slope), got = tiled(
        inner, (ff // f_tile, rows // r_tile),
        [
            (normed, (r_tile, model), lambda j, i: (i, 0)),
            (up_w, (model, f_tile), lambda j, i: (0, j)),
            (b_fc1[None], (1, f_tile), lambda j, i: (0, j)),
        ],
        [out, out], carry, 48)
    return value, slope, got


def hidden_grad(cot, down_w, slope, r_tile, f_tile, carry, adds):
    rows, model = cot.shape
    ff = down_w.shape[0]
    grid = (ff // f_tile, rows // r_tile)
    extra_in, extra_out = side_sums(adds, grid)

    def inner(c_ref, w_ref, s_ref, *refs):
        sides, (g_ref, b_ref, *results) = refs[: len(extra_in)], refs[len(extra_in) :]
        for n in range(len(adds)):
            results[n][...] = add_low(sides[2 * n][...], sides[2 * n + 1][...])
        low = (dot_nt(c_ref[...], w_ref[...]) * s_ref[...].astype(f32)).astype(bf16)
        g_ref[...] = low
        part = jnp.sum(low.astype(f32).reshape(r_tile // 8, 8, f_tile), axis=0)

        @pl.when(pl.program_id(1) == 0)
        def _():
            b_ref[...] = part

        @pl.when(pl.program_id(1) > 0)
        def _():
            b_ref[...] += part

    (grad, sums, *results), got = tiled(
        inner, grid,
        [
            (cot, (r_tile, model), lambda j, i: (i, 0)),
            (down_w, (f_tile, model), lambda j, i: (j, 0)),
            (slope, (r_tile, f_tile), lambda j, i: (i, j)),
        ] + extra_in,
        [
            ((rows, ff), bf16, (r_tile, f_tile), lambda j, i: (i, j)),
            ((8, ff), f32, (8, f_tile), lambda j, i: (0, j)),
        ] + extra_out, carry)
    return grad, sums, results, got


def norm_gather(tokens, ln_gain, ln_bias, tag):
    local, model = tokens.shape
    half, tile = local // 2, local // 6

    def kernel(x_ref, gain_ref, bias_ref, all_ref, mine, sems):
        meet([("tensor", 1), ("tensor", 2)])
        part = lambda n: mine.at[pl.ds(n * half, half)]
        rows = lambda at, size: all_ref.at[pl.ds(at, size)]
        copies = remote_copies([
            (part(1), rows(local + half, half), "tensor", 1),
            (part(0), rows(2 * local, half), "tensor", 2),
            (part(0), rows(local, half), "tensor", 1),
            (part(1), rows(2 * local + half, half), "tensor", 2),
            (rows(2 * local, half), rows(3 * local, half), "tensor", 1),
            (rows(local + half, half), rows(3 * local + half, half), "tensor", 2),
            (mine, rows(0, local), None, 0),
        ], sems)

        def normalize(n):
            @pl.loop(0, 3)
            def _(i):
                at = pl.ds(pl.multiple_of(n * half + i * tile, tile), tile)
                xhat, inverse = norm_parts(x_ref[at, :].astype(f32))
                mine[at, :] = (xhat * gain_ref[...] + bias_ref[...]).astype(bf16)

        normalize(1)
        copies[0].start()
        normalize(0)
        for n in (1, 2, 3, 6):
            copies[n].start()
        copies[1].wait_recv()
        copies[4].start()
        copies[0].wait_recv()
        copies[5].start()
        copies[0].wait_send()
        copies[1].wait_send()
        for n in (2, 3, 4, 5, 6):
            copies[n].wait()

    return pl.pallas_call(
        kernel,
        in_specs=[pl.BlockSpec(memory_space=pltpu.VMEM)] * 3,
        out_specs=pl.BlockSpec(memory_space=pltpu.HBM),
        out_shape=jax.ShapeDtypeStruct((4 * local, model), bf16),
        scratch_shapes=[pltpu.VMEM((local, model), bf16), pltpu.SemaphoreType.DMA((2, 7))],
        compiler_params=pltpu.CompilerParams(
            vmem_limit_bytes=63 << 20, collective_id=tag, has_side_effects=True),
        cost_estimate=hint(),
    )(tokens, ln_gain[None], ln_bias[None])


def gather_sides(x, tag):
    local, model = x.shape
    return Carry(
        tag, [x], [((4 * local, model), bf16)],
        lambda src, dst: [
            (src[0], dst[0].at[pl.ds(local, local)], "tensor", 1),
            (src[0], dst[0].at[pl.ds(2 * local, local)], "tensor", 2),
            (src[0], dst[0].at[pl.ds(0, local)], None, 0),
        ], 3)


def gather_corner(whole, tag):
    local = whole.shape[0] // 4
    half = local // 2
    return Carry(
        tag, [whole], [(whole.shape, bf16)],
        lambda src, dst: [
            (dst[0].at[pl.ds(2 * local, half)], dst[0].at[pl.ds(3 * local, half)], "tensor", 1),
            (dst[0].at[pl.ds(local + half, half)], dst[0].at[pl.ds(3 * local + half, half)], "tensor", 2),
        ], 2, True)


def norm_back(own, low_parts, high_parts, tokens, cotangent, ln_gain):
    rows, model = tokens.shape
    tiles = 6
    tile = rows // tiles
    half = tiles // 2

    def inner(own_low, own_high, l0, l1, h0, h1, t_ref, c_ref, gain_ref, o_ref, s_ref):
        step = pl.program_id(0)

        def compute(a, b, c):
            grad = a[...].astype(f32) + b[...].astype(f32) + c[...].astype(f32)
            cot = c_ref[...].astype(f32)
            xhat, inverse = norm_parts(t_ref[...].astype(f32))
            scaled = grad * gain_ref[...]
            both = grad * xhat
            o_ref[...] = cot + inverse * (
                scaled
                - jnp.mean(scaled, axis=-1, keepdims=True)
                - xhat * jnp.mean(scaled * xhat, axis=-1, keepdims=True))
            terms = [jnp.sum(v.reshape(tile // 8, 8, model), axis=0) for v in (both, grad, cot)]

            @pl.when(step == 0)
            def _():
                for n in range(3):
                    s_ref[n] = terms[n]

            @pl.when(step > 0)
            def _():
                for n in range(3):
                    s_ref[n] += terms[n]

        @pl.when(step < half)
        def _():
            compute(own_low, l0, l1)

        @pl.when(step >= half)
        def _():
            compute(own_high, h0, h1)

    low = lambda i: (jnp.minimum(i, half - 1), 0)
    high = lambda i: (jnp.maximum(i - half, 0), 0)
    each = lambda i: (i, 0)
    block = (tile, model)
    (grad, sums), ignored = tiled(
        inner, (tiles,),
        [(own[0], block, low), (own[1], block, high)]
        + [(a, block, low) for a in low_parts] + [(a, block, high) for a in high_parts]
        + [(tokens, block, each), (cotangent, block, each), (ln_gain[None], (1, model), lambda i: (0, 0))],
        [((rows, model), f32, block, each), ((3, 8, model), f32, (3, 8, model), lambda i: (0, 0, 0))])
    return grad, jnp.sum(sums, axis=1)


def norm_parts(rows_in):
    row_mean = jnp.mean(rows_in, axis=-1, keepdims=True)
    centred = rows_in - row_mean
    inverse = lax.rsqrt(jnp.mean(centred * centred, axis=-1, keepdims=True) + norm_eps)
    return centred * inverse, inverse


def gelu_parts(v):
    scale = (2.0 / jnp.pi) ** 0.5
    square = v * v
    t = jnp.tanh(v * (scale + (scale * 0.044715) * square))
    half = 0.5 * (1.0 + t)
    slope = half + (half * (1.0 - t)) * (v * (scale + (scale * 3 * 0.044715) * square))
    return v * half, slope


def body(
    tokens,
    cotangent,
    ln_gain,
    ln_bias,
    w_qkv,
    b_qkv,
    w_out,
    w_fc1,
    b_fc1,
    w_fc2,
    resid_bias,
    parents,
):
    size = lax.axis_size("tensor")
    groups = lax.axis_size("dp")
    local_rows, model = tokens.shape
    me = lax.axis_index("tensor")
    width = w_qkv.shape[2]
    four = size == 4
    t1, t2 = ("tensor", 1), ("tensor", 2)
    half_cols = model // 2

    tables = rope_tables()
    up_w = lax.all_gather(w_fc1, "dp", axis=0, tiled=True)
    w_heads = jnp.concatenate([w_qkv, jnp.transpose(w_out)[None]], axis=0)
    heads_w = lax.all_gather(w_heads, "dp", axis=1, tiled=True)
    down_w = lax.all_gather(w_fc2, "dp", axis=1, tiled=True)
    if four:
        normed = norm_gather(tokens, ln_gain, ln_bias, 1)
    else:
        normed_local = (norm_parts(tokens.astype(f32))[0] * ln_gain + ln_bias).astype(bf16)
        normed, cot_full = (
            jnp.concatenate([x] + [xor_send(x, i, size) for i in range(1, size)], axis=0)
            for x in (normed_local, cotangent))
    activated, slope, got = hidden_forward(
        normed, up_w, b_fc1, local_rows, half_cols, gather_sides(cotangent, 2) if four else None)
    if four:
        cot_full = tiled(None, (), [], [], gather_corner(got[0], 3))[1][0]
    projected = (
        jnp.einsum(
            "td,cdh->cth", after(normed, activated, cot_full), heads_w[:3], preferred_element_type=f32)
        + b_qkv[:, None, :]
    ).astype(bf16)
    grad_w_fc2 = dot_tn(after(activated, projected), cot_full).astype(bf16)
    summed_fc2 = lax.psum_scatter(grad_w_fc2, "dp", scatter_dimension=1, tiled=True)
    grad_attended = dot_nn(after(cot_full, grad_w_fc2), heads_w[3]).astype(bf16)
    attended, grad_qkv, aux = attention(parents[0], me[None], size, *tables, projected, grad_attended)

    branch, ignored = chunk_matmul(
        [(attended, heads_w, -1, 3), (activated, down_w, -1, None)],
        model, half_cols, size, size, lambda i: i, cut=2)
    grad_w_heads, got = head_grads(
        after(normed, branch[0]), grad_qkv, cot_full, attended, half_cols,
        sending(4, (branch[6],) + t1, (branch[7],) + t2) if four else None)
    summed_heads = lax.psum_scatter(grad_w_heads, "dp", scatter_dimension=1, tiled=True)
    grad_hidden, sums_fc1, branch_next, side = hidden_grad(
        after(cot_full, grad_w_heads), down_w, slope, local_rows, half_cols,
        sending(5, (branch[2],) + t1, (branch[5],) + t2) if four else None,
        [(branch[3], got[1]), (branch[4], got[0])] if four else [])
    dp_bits = range(1, groups)
    backs = [(grad_qkv, heads_w, c, c) for c in range(3)] + [(after(grad_hidden, summed_fc2), up_w, -1, -1)]
    if four:
        far, last = chunk_matmul(
            backs, model, half_cols, 8, 4, lambda i: 7 - i - 2 * (i // 3),
            sending(6, (branch_next[0],) + t1, (branch_next[1],) + t2))
        branch_sum = [
            branch[0].astype(f32) + side[0].astype(f32) + last[1].astype(f32),
            branch[1].astype(f32) + last[0].astype(f32) + side[1].astype(f32)]
        grad_w_fc1, got = weight_grad(
            after(normed, far[7]), grad_hidden, half_cols, half_cols,
            sending(
                7, (far[6],) + t1, (far[7],) + t2,
                *[(aux, "dp", bits) for bits in dp_bits], *[(sums_fc1, "dp", bits) for bits in dp_bits]))
        all_aux = [aux] + got[2 : 1 + groups]
        all_fc1 = [sums_fc1] + got[1 + groups :]
        backs[3] = (after(grad_hidden, grad_w_fc1),) + backs[3][1:]
        near, side = chunk_matmul(
            backs, model, half_cols, 8, 4, lambda i: 4 - i - i // 2,
            sending(8, (far[2],) + t1, (far[5],) + t2), {3: got[1], 4: got[0]})
        one, two = xor_send(near[3], 1, size), xor_send(near[4], 2, size)
        input_grad, terms = norm_back(
            [near[0], near[1]], [side[0], two], [one, side[1]], tokens, cotangent, ln_gain)
        branch_sum[0] = after(branch_sum[0], near[0])
        all_aux[0] = after(aux, near[0])
        all_fc1[0] = after(sums_fc1, near[0])
    else:
        parts, ignored = chunk_matmul(backs, model, half_cols, size, size, lambda i: i, cut=2)
        grad_w_fc1, ignored = weight_grad(normed, grad_hidden, half_cols, half_cols, None)
        all_aux, all_fc1 = (list(lax.all_gather(x, "dp")) for x in (aux, sums_fc1))
        branch_sum = scatter_rest(branch, size)
        grad_normed = jnp.concatenate(scatter_rest(parts, size), axis=0)
        xhat, inverse = norm_parts(tokens.astype(f32))
        grad_xhat = grad_normed * ln_gain
        cot_local = cotangent.astype(f32)
        input_grad = cot_local + inverse * (
            grad_xhat
            - jnp.mean(grad_xhat, axis=-1, keepdims=True)
            - xhat * jnp.mean(grad_xhat * xhat, axis=-1, keepdims=True)
        )
        terms = jnp.stack(
            [jnp.sum(grad_normed * xhat, axis=0), jnp.sum(grad_normed, axis=0), jnp.sum(cot_local, axis=0)]
        )
    summed_fc1 = lax.psum_scatter(grad_w_fc1, "dp", scatter_dimension=0, tiled=True)
    output_rows = (
        tokens.astype(f32) + jnp.concatenate(branch_sum, axis=0) + resid_bias).astype(bf16)
    summed_fc1, summed_heads, summed_fc2 = (
        w.astype(f32) for w in (summed_fc1, summed_heads, summed_fc2))
    summed_qkv, summed_out = summed_heads[:3], jnp.transpose(summed_heads[3])

    bias_qkv = jnp.transpose(sum(a[:, :3] for a in all_aux), (1, 0, 2)).reshape(3, width)
    bias_fc1 = jnp.sum(sum(all_fc1), axis=0)
    head_top = functools.reduce(jnp.maximum, [a[:, 3:5, 0] for a in all_aux]).reshape(-1)
    factor = jnp.sqrt(clip_tau / jnp.maximum(head_top, clip_tau))
    clipped_qk = (w_qkv[:2].astype(f32) * jnp.repeat(factor, HDIM)[None, None, :]).astype(bf16)

    every = size * groups
    pieces = jnp.transpose(terms.reshape(3, every, model // every), (1, 0, 2)).reshape(every, -1)
    pieces = lax.all_to_all(pieces, ("dp", "tensor"), 0, 0, tiled=True)
    grad_small = jnp.sum(pieces, axis=0).reshape(3, model // every)
    return (
        output_rows,
        input_grad,
        grad_small,
        summed_qkv,
        bias_qkv,
        summed_out,
        summed_fc1,
        bias_fc1,
        summed_fc2,
        clipped_qk,
    )


def solution(mesh):
    return jax.shard_map(
        body,
        mesh=mesh,
        in_specs=(
            P(("dp", "tensor"), None),
            P(("dp", "tensor"), None),
            P(),
            P(),
            P(None, "dp", "tensor"),
            P(None, "tensor"),
            P("tensor", "dp"),
            P("dp", "tensor"),
            P("tensor"),
            P("tensor", "dp"),
            P(),
            P("dp", None),
        ),
        out_specs=(
            P(("dp", "tensor"), None),
            P(("dp", "tensor"), None),
            P(None, ("dp", "tensor")),
            P(None, "dp", "tensor"),
            P(None, "tensor"),
            P("tensor", "dp"),
            P("dp", "tensor"),
            P("tensor"),
            P("tensor", "dp"),
            P(None, "dp", "tensor"),
        ),
        check_vma=False,
    )
```

```python
import functools

import jax
import jax.numpy as jnp
import numpy as np
from jax import lax
from jax.experimental import pallas as pl
from jax.experimental.pallas import tpu as pltpu
from jax.sharding import PartitionSpec as P

HDIM = 64
ROT = 32
SEG = 128
TRUNK = 6
BRANCHES = 4
LEAVES = 2
TREE_SEGS = TRUNK + BRANCHES + BRANCHES * LEAVES
bf16 = jnp.bfloat16
f32 = jnp.float32
NEG = -1e30
rope_base = 10000.0


def dot_nn(a, b):
    return lax.dot_general(a, b, (((1,), (0,)), ((), ())), preferred_element_type=f32)


def dot_nt(a, b):
    return lax.dot_general(a, b, (((1,), (1,)), ((), ())), preferred_element_type=f32)


def rope_tables():
    lane = np.arange(2 * HDIM) % HDIM
    freq = np.where(lane < ROT, rope_base ** (-2.0 * (lane % (ROT // 2)) / ROT), 0.0)
    angles = np.concatenate([np.arange(SEG), SEG * np.arange(TRUNK + 2)])[:, None] * freq[None, :]
    return np.cos(angles).astype(np.float32), np.sin(angles).astype(np.float32)


def partner(x):
    lane = lax.broadcasted_iota(jnp.int32, x.shape, 1) % HDIM
    half = ROT // 2
    return jnp.where(lane < half, pltpu.roll(x, 2 * HDIM - half, 1), pltpu.roll(x, half, 1))


def attn_kernel(size, par, me, cos_in, sin_in, qkv_ref, do_in, att_ref, g_ref, aux_ref,
                qs, kr, vr, do_ref, kt, vt, dot_t, att, dqn, dk, dv, s_ref, top, cos_ref, sin_ref):
    rows = TREE_SEGS * SEG
    step = 2 * SEG
    local = rows // size
    lane_low = lax.broadcasted_iota(jnp.int32, (step, 2 * HDIM), 1) < HDIM

    def unit(n):
        return jnp.where(
            lax.broadcasted_iota(jnp.int32, (n, n), 0) == lax.broadcasted_iota(jnp.int32, (n, n), 1),
            1.0, 0.0).astype(bf16)

    unit_wide = unit(2 * HDIM)

    def places(i):
        here = pl.ds(i * local, local)
        there = pl.ds(pl.multiple_of((me[0] ^ i) * local, local), local)
        return here, there

    @pl.when(pl.program_id(0) == 0)
    def _():
        sign = jnp.where(lax.broadcasted_iota(jnp.int32, (SEG, 2 * HDIM), 1) % HDIM < ROT // 2, -1.0, 1.0)
        cos_place, sin_place = cos_in[:SEG, :], sin_in[:SEG, :]
        for depth in range(TRUNK + 2):
            cos_seg, sin_seg = cos_in[SEG + depth : SEG + depth + 1, :], sin_in[SEG + depth : SEG + depth + 1, :]
            cos = cos_place * cos_seg - sin_place * sin_seg
            sin = (sin_place * cos_seg + cos_place * sin_seg) * sign
            first = [depth] if depth < TRUNK else range(TRUNK, TRUNK + BRANCHES)
            for seg in first if depth <= TRUNK else range(TRUNK + BRANCHES, TREE_SEGS):
                cos_ref[seg * SEG : (seg + 1) * SEG, :] = cos
                sin_ref[seg * SEG : (seg + 1) * SEG, :] = sin

    for i in range(size):
        here, there = places(i)
        cos, sin = cos_ref[there, :], sin_ref[there, :]
        q = qkv_ref[0, here, :].astype(f32)
        k = qkv_ref[1, here, :].astype(f32)
        qs[there, :] = ((q * cos + partner(q) * sin) * (HDIM ** -0.5)).astype(bf16)
        kr[there, :] = (k * cos + partner(k) * sin).astype(bf16)
        vr[there, :] = qkv_ref[2, here, :]
        do_ref[there, :] = do_in[here, :]

    for i in range(rows // step):
        at = pl.ds(i * step, step)
        kt[:, at] = dot_nt(unit_wide, kr[at, :]).astype(bf16)
        vt[:, at] = dot_nt(unit_wide, vr[at, :]).astype(bf16)
        dot_t[:, at] = dot_nt(unit_wide, do_ref[at, :]).astype(bf16)
        dk[at, :] = jnp.zeros((step, 2 * HDIM), f32)
        dv[at, :] = jnp.zeros((step, 2 * HDIM), f32)

    top[...] = jnp.full((2, 8, step), NEG, f32)
    key_id = lax.broadcasted_iota(jnp.int32, (SEG, step), 0)
    query_id = lax.broadcasted_iota(jnp.int32, (SEG, step), 1) % SEG
    pair_mask = key_id <= query_id
    tri_mask = lax.broadcasted_iota(jnp.int32, (step, step), 0) <= lax.broadcasted_iota(
        jnp.int32, (step, step), 1)

    def seg_at(start, size):
        if isinstance(start, int):
            return pl.ds(start, size)
        return pl.ds(pl.multiple_of(start, SEG), size)

    def block(q0, q1, chunks, diag):
        halves = [seg_at(q0, SEG), seg_at(q1, SEG)]
        q_all = jnp.concatenate([qs[halves[0], :], qs[halves[1], :]], axis=0)
        do_all = jnp.concatenate([do_ref[halves[0], :], do_ref[halves[1], :]], axis=0)
        zero = jnp.zeros_like(q_all)
        pieces = []
        off = 0
        for start, size in chunks:
            pieces.append((off, start, size, 'full'))
            off += size
        pieces.append((off, q0, step, 'tri') if diag else (off, None, SEG, 'pair'))
        both = range(2)
        qh = [jnp.where(lane_low if h == 0 else ~lane_low, q_all, zero) for h in both]
        dh = [jnp.where(lane_low if h == 0 else ~lane_low, do_all, zero) for h in both]
        q_stack = jnp.concatenate(qh, axis=0)
        d_stack = jnp.concatenate(dh, axis=0)

        def part(x, i):
            return x[i * SEG:(i + 1) * SEG]

        def lanes(x, i):
            return x[:, i * SEG:(i + 1) * SEG]

        def left(ref, piece, stack):
            o, start, size, kind = piece
            if kind == 'pair':
                each = [
                    dot_nt(ref[halves[i], :], jnp.concatenate([part(stack, i), part(stack, 2 + i)], axis=0))
                    for i in both]
                return [jnp.concatenate([lanes(x, h) for x in each], axis=1) for h in both]
            x = dot_nt(ref[seg_at(start, size), :], stack)
            return [x[:, h * step : (h + 1) * step] for h in both]

        def turned(ref, h, piece, x):
            o, start, size, kind = piece
            rows_h = slice(h * HDIM, (h + 1) * HDIM)
            if kind == 'pair':
                return jnp.concatenate(
                    [dot_nn(ref[rows_h, halves[i]], lanes(x, i)) for i in both], axis=1)
            return dot_nn(ref[rows_h, seg_at(start, size)], x)

        def add_rows(ref, piece, xs, stack):
            o, start, size, kind = piece
            if kind == 'pair':
                for i in both:
                    ref[halves[i], :] += dot_nn(
                        jnp.concatenate([lanes(x, i) for x in xs], axis=1),
                        jnp.concatenate([part(stack, i), part(stack, 2 + i)], axis=0))
            else:
                ref[seg_at(start, size), :] += dot_nn(jnp.concatenate(xs, axis=1), stack)

        def fold(x, op):
            return op(x.reshape(x.shape[0] // 8, 8, step), axis=0)

        tops = [[], []]
        sums = [[], []]
        for piece in pieces:
            o, start, size, kind = piece
            scores = left(kr, piece, q_stack)
            for h in both:
                s = scores[h]
                if kind == 'tri':
                    s = jnp.where(tri_mask, s, NEG)
                if kind == 'pair':
                    s = jnp.where(pair_mask, s, NEG)
                m = fold(s, jnp.max)
                top[h] = jnp.maximum(top[h], m)
                m = jnp.max(m, axis=0, keepdims=True)
                e = jnp.exp(s - m)
                s_ref[h, o:o + size, :] = e
                tops[h].append(m)
                sums[h].append(jnp.sum(fold(e, jnp.sum), axis=0, keepdims=True))
        scales = []
        for h in both:
            m = functools.reduce(jnp.maximum, tops[h])
            w = [jnp.exp(mc - m) for mc in tops[h]]
            inv = 1.0 / sum(wc * sc for wc, sc in zip(w, sums[h]))
            scales.append([wc * inv for wc in w])
        o_acc = [jnp.zeros((HDIM, step), f32)] * 2
        for n, piece in enumerate(pieces):
            o, start, size, kind = piece
            low = []
            for h in both:
                p = s_ref[h, o:o + size, :] * scales[h][n]
                s_ref[h, o:o + size, :] = p
                low.append(p.astype(bf16))
                o_acc[h] = o_acc[h] + turned(vt, h, piece, low[h])
            add_rows(dv, piece, low, d_stack)
        deltas = []
        for h in both:
            d_turned = jnp.concatenate(
                [dot_t[h * HDIM:(h + 1) * HDIM, halves[i]] for i in both], axis=1)
            deltas.append(jnp.sum(o_acc[h] * d_turned.astype(f32), axis=0, keepdims=True))
        dq_acc = [jnp.zeros((HDIM, step), f32)] * 2
        for n, piece in enumerate(pieces):
            o, start, size, kind = piece
            low = []
            dps = left(vr, piece, d_stack)
            for h in both:
                low.append((s_ref[h, o:o + size, :] * (dps[h] - deltas[h])).astype(bf16))
                dq_acc[h] = dq_acc[h] + turned(kt, h, piece, low[h])
            add_rows(dk, piece, low, q_stack)
        o_rows = jnp.concatenate(o_acc, axis=0).T.astype(bf16)
        dq_rows = jnp.concatenate(dq_acc, axis=0).T
        for i in both:
            att[halves[i], :] = part(o_rows, i)
            dqn[halves[i], :] = part(dq_rows, i)

    for b in range(TRUNK // 2):
        block(b * step, b * step + SEG, [(c * step, step) for c in range(b)], True)
    trunk_chunks = [(c * step, step) for c in range(TRUNK // 2)]

    @pl.loop(0, BRANCHES // 2)
    def _(i):
        start = (TRUNK + 2 * i) * SEG
        block(start, start + SEG, trunk_chunks, False)

    @pl.loop(0, BRANCHES)
    def _(i):
        branch = TRUNK + i
        first = TREE_SEGS - 1
        last = TRUNK + BRANCHES
        for leaf in range(TREE_SEGS - 1, TRUNK + BRANCHES - 1, -1):
            first = jnp.where(par[leaf] == branch, leaf, first)
        for leaf in range(TRUNK + BRANCHES, TREE_SEGS):
            last = jnp.where(par[leaf] == branch, leaf, last)
        block(first * SEG, last * SEG, trunk_chunks + [(branch * SEG, SEG)], False)

    totals = [jnp.zeros((8, 2 * HDIM), f32)] * 3
    for i in range(size):
        here, there = places(i)
        cos, sin = cos_ref[there, :], sin_ref[there, :]
        att_ref[here, :] = att[there, :]
        dq = dqn[there, :] * (HDIM ** -0.5)
        dkr = dk[there, :]
        parts = [dq * cos - partner(dq) * sin, dkr * cos - partner(dkr) * sin, dv[there, :]]
        for c in range(3):
            low = parts[c].astype(bf16)
            g_ref[c, here, :] = low
            totals[c] = totals[c] + jnp.sum(low.astype(f32).reshape(local // 8, 8, 2 * HDIM), axis=0)

    rows_out = [jnp.sum(t, axis=0, keepdims=True) for t in totals]
    for h in range(2):
        rows_out.append(jnp.full((1, 2 * HDIM), jnp.max(top[h]), f32))
    rows_out.append(jnp.zeros((3, 2 * HDIM), f32))
    aux_ref[0] = jnp.concatenate(rows_out, axis=0)


def attention(parents, me, size, cos, sin, qkv, grad_att):
    rows, width = grad_att.shape
    pairs = width // (2 * HDIM)
    step = 2 * SEG
    wide = 2 * HDIM
    keys = TRUNK * SEG + 2 * SEG
    blk = lambda: pl.BlockSpec((rows, wide), lambda p, par, me: (0, p))
    blk3 = lambda: pl.BlockSpec((3, rows, wide), lambda p, par, me: (0, 0, p))
    tab = lambda: pl.BlockSpec((SEG + TRUNK + 2, wide), lambda p, par, me: (0, 0))
    return pl.pallas_call(
        functools.partial(attn_kernel, size),
        out_shape=(
            jax.ShapeDtypeStruct((rows, width), bf16),
            jax.ShapeDtypeStruct((3, rows, width), bf16),
            jax.ShapeDtypeStruct((pairs, 8, wide), f32),
        ),
        grid_spec=pltpu.PrefetchScalarGridSpec(
            num_scalar_prefetch=2,
            grid=(pairs,),
            in_specs=[tab(), tab(), blk3(), blk()],
            out_specs=[blk(), blk3(), pl.BlockSpec((1, 8, wide), lambda p, par, me: (p, 0, 0))],
            scratch_shapes=[
                pltpu.VMEM((rows, wide), bf16),
                pltpu.VMEM((rows, wide), bf16),
                pltpu.VMEM((rows, wide), bf16),
                pltpu.VMEM((rows, wide), bf16),
                pltpu.VMEM((wide, rows), bf16),
                pltpu.VMEM((wide, rows), bf16),
                pltpu.VMEM((wide, rows), bf16),
                pltpu.VMEM((rows, wide), bf16),
                pltpu.VMEM((rows, wide), f32),
                pltpu.VMEM((rows, wide), f32),
                pltpu.VMEM((rows, wide), f32),
                pltpu.VMEM((2, keys, step), f32),
                pltpu.VMEM((2, 8, step), f32),
                pltpu.VMEM((rows, wide), f32),
                pltpu.VMEM((rows, wide), f32),
            ],
        ),
        compiler_params=pltpu.CompilerParams(
            dimension_semantics=("arbitrary",), vmem_limit_bytes=63 << 20),
        cost_estimate=pl.CostEstimate(flops=60 * 10**9, transcendentals=17 * 10**6, bytes_accessed=24 << 20),
    )(parents, me, cos, sin, qkv, grad_att)


clip_tau = 10.0
norm_eps = 1e-05


def dot_tn(a, b):
    return lax.dot_general(a, b, (((0,), (0,)), ((), ())), preferred_element_type=f32)


def xor_send(x, bits, size):
    return lax.ppermute(x, "tensor", [(i, i ^ bits) for i in range(size)])


def add_low(a, b):
    return (a.astype(f32) + b.astype(f32)).astype(bf16)


def scatter_rest(parts, size):
    low, high = parts[0].astype(f32), parts[1].astype(f32)
    for i in range(1, size):
        low = low + xor_send(parts[2 * i], i, size).astype(f32)
        high = high + xor_send(parts[2 * i + 1], i, size).astype(f32)
    return [low, high]


def after(x, *others):
    return lax.optimization_barrier((x,) + others)[0]


class Carry:
    def __init__(self, tag=0, arrays=(), shapes=(), links=None, count=0, alias=False):
        self.tag, self.arrays, self.links, self.count, self.alias = tag, list(arrays), links, count, alias
        self.shapes = [jax.ShapeDtypeStruct(*shape) for shape in shapes]


def sending(tag, *sends):
    return Carry(
        tag, [a for a, axis, bits in sends], [(a.shape, a.dtype) for a, axis, bits in sends],
        lambda src, dst: [(src[n], dst[n], axis, bits) for n, (a, axis, bits) in enumerate(sends)], len(sends))


def other_device(axis, bits):
    t = lax.axis_index(axis)
    at = t
    for n in range(8):
        if bits >> n & 1:
            at = at + (1 << n) - (2 << n) * ((t // (1 << n)) % 2)
    return {axis: at}


def meet(partners):
    barrier = pltpu.get_barrier_semaphore()
    for axis, bits in partners:
        pl.semaphore_signal(
            barrier, inc=1, device_id=other_device(axis, bits), device_id_type=pl.DeviceIdType.MESH)
    pl.semaphore_wait(barrier, len(partners))


def remote_copies(links, sems):
    return [
        pltpu.make_async_copy(src, dst, sems.at[0, n])
        if axis is None
        else pltpu.make_async_remote_copy(
            src_ref=src,
            dst_ref=dst,
            send_sem=sems.at[0, n],
            recv_sem=sems.at[1, n],
            device_id=other_device(axis, bits),
            device_id_type=pl.DeviceIdType.MESH,
        )
        for n, (src, dst, axis, bits) in enumerate(links)
    ]


def hint():
    return pl.CostEstimate(flops=10**10, transcendentals=0, bytes_accessed=2 << 20)


def tiled(inner, grid, ins, outs, carry=None, vmem=63):
    carry = carry or Carry()
    n_in, n_out, n_src, n_dst = len(ins), len(outs), len(carry.arrays), len(carry.shapes)
    in_specs = [pl.BlockSpec(block, at) for a, block, at in ins]
    out_specs = [pl.BlockSpec(block, at) for shape, dtype, block, at in outs]
    any_spec = pl.BlockSpec(memory_space=pltpu.HBM)
    arrays = [a for a, block, at in ins]
    shapes = [jax.ShapeDtypeStruct(shape, dtype) for shape, dtype, block, at in outs]
    if not carry.count:
        results = pl.pallas_call(
            inner, grid=grid, in_specs=in_specs, out_specs=out_specs, out_shape=shapes,
            compiler_params=pltpu.CompilerParams(
                dimension_semantics=("arbitrary",) * len(grid), vmem_limit_bytes=vmem << 20),
            cost_estimate=hint(),
        )(*arrays)
        return list(results), []

    def kernel(*refs):
        sources = refs[n_in : n_in + n_src]
        places = refs[n_in + n_src : n_in + n_src + n_out]
        targets = refs[n_in + n_src + n_out : -1]
        links = carry.links(sources, targets)
        meet(sorted(set((axis, bits) for src, dst, axis, bits in links if axis is not None)))
        copies = remote_copies(links, refs[-1])
        for copy in copies:
            copy.start()
        if grid:
            pltpu.emit_pipeline(inner, grid=grid, in_specs=in_specs, out_specs=out_specs)(*refs[:n_in], *places)
        for copy in copies:
            copy.wait()

    results = pl.pallas_call(
        kernel,
        in_specs=[any_spec] * (n_in + n_src),
        out_specs=[any_spec] * (n_out + n_dst),
        out_shape=shapes + carry.shapes,
        scratch_shapes=[pltpu.SemaphoreType.DMA((2, carry.count))],
        input_output_aliases={n_in: n_out} if carry.alias else {},
        compiler_params=pltpu.CompilerParams(
            vmem_limit_bytes=vmem << 20, collective_id=carry.tag, has_side_effects=True),
        cost_estimate=hint(),
    )(*arrays, *carry.arrays)
    return list(results[:n_out]), list(results[n_out:])


def side_sums(adds, grid):
    at = lambda j, i: (0, j * grid[1] + i)
    block = lambda a: (a.shape[0], a.shape[1] // (grid[0] * grid[1]))
    ins = [(a, block(a), at) for pair in adds for a in pair]
    outs = [(a.shape, a.dtype, block(a), at) for a, b in adds]
    return ins, outs


def chunk_matmul(pairs, columns, tile, count, blocks, at, carry=None, adds=(), cut=1):
    local = pairs[0][0].shape[-2] // count
    grid = (columns // tile, blocks)
    ins = []
    for x, w, c, d in pairs:
        depth = x.shape[-1]
        if c < 0:
            ins.append((x, (local, depth), lambda j, i: (at(i), 0)))
        else:
            ins.append((x, (None, local, depth), lambda j, i, c=c: (c, at(i), 0)))
        if d is None:
            ins.append((w, (depth, tile), lambda j, i: (0, j)))
        elif d < 0:
            ins.append((w, (tile, depth), lambda j, i: (j, 0)))
        else:
            ins.append((w, (None, tile, depth), lambda j, i, d=d: (d, j, 0)))
    terms = len(pairs)
    adds = dict(adds)
    more = [(adds[b], (local, tile), lambda j, i: (0, j)) for b in sorted(adds)]
    part = local // cut
    outs = [((part, columns), bf16, (part, tile), lambda j, i: (0, j))] * (blocks * cut)

    def inner(*refs):
        sides, results = dict(zip(sorted(adds), refs[2 * terms :])), refs[2 * terms + len(more) :]
        acc = None
        for n in range(terms):
            dot = dot_nn if pairs[n][3] is None else dot_nt
            term = dot(refs[2 * n][...], refs[2 * n + 1][...])
            acc = term if acc is None else acc + term
        for i in range(blocks):
            @pl.when(pl.program_id(1) == i)
            def _(i=i):
                whole = acc
                if at(i) in sides:
                    whole = whole + sides[at(i)][...].astype(f32)
                low = whole.astype(bf16)
                for n in range(cut):
                    results[i * cut + n][...] = low[n * part : (n + 1) * part]

    results, got = tiled(inner, grid, ins + more, outs, carry)
    return {at(i) * cut + n: results[i * cut + n] for i in range(blocks) for n in range(cut)}, got


def qkv_grads(normed, grad_qkv, tile, carry):
    rows, model = normed.shape
    width = grad_qkv.shape[2]

    def inner(n_ref, g_ref, o_ref):
        o_ref[...] = dot_tn(n_ref[...], g_ref[...]).astype(bf16)

    (grads,), got = tiled(
        inner, (3, model // tile),
        [
            (normed, (rows, tile), lambda c, i: (0, i)),
            (grad_qkv, (None, rows, width), lambda c, i: (c, 0, 0)),
        ],
        [((3, model, width), bf16, (None, tile, width), lambda c, i: (c, i, 0))], carry)
    return grads, got


def weight_grad(x, y, m_tile, n_tile, carry):
    rows, m = x.shape
    n = y.shape[1]

    def inner(x_ref, y_ref, o_ref):
        o_ref[...] = dot_tn(x_ref[...], y_ref[...]).astype(bf16)

    (grad,), got = tiled(
        inner, (m // m_tile, n // n_tile),
        [(x, (rows, m_tile), lambda i, j: (0, i)), (y, (rows, n_tile), lambda i, j: (0, j))],
        [((m, n), bf16, (m_tile, n_tile), lambda i, j: (i, j))], carry)
    return grad, got


def hidden_forward(normed, up_w, b_fc1, r_tile, f_tile, carry):
    rows, model = normed.shape
    ff = up_w.shape[1]

    def inner(n_ref, w_ref, b_ref, a_ref, s_ref):
        value, slope = gelu_parts(dot_nn(n_ref[...], w_ref[...]) + b_ref[...])
        a_ref[...] = value.astype(bf16)
        s_ref[...] = slope.astype(bf16)

    out = ((rows, ff), bf16, (r_tile, f_tile), lambda j, i: (i, j))
    (value, slope), got = tiled(
        inner, (ff // f_tile, rows // r_tile),
        [
            (normed, (r_tile, model), lambda j, i: (i, 0)),
            (up_w, (model, f_tile), lambda j, i: (0, j)),
            (b_fc1[None], (1, f_tile), lambda j, i: (0, j)),
        ],
        [out, out], carry, 48)
    return value, slope, got


def project(normed, qkv_w, b_qkv, r_tile, carry):
    rows, model = normed.shape
    width = qkv_w.shape[2]

    def inner(n_ref, w_ref, b_ref, o_ref):
        o_ref[...] = (dot_nn(n_ref[...], w_ref[...]) + b_ref[...]).astype(bf16)

    (out,), got = tiled(
        inner, (3, rows // r_tile),
        [
            (normed, (r_tile, model), lambda c, i: (i, 0)),
            (qkv_w, (None, model, width), lambda c, i: (c, 0, 0)),
            (b_qkv[:, None], (None, 1, width), lambda c, i: (c, 0, 0)),
        ],
        [((3, rows, width), bf16, (None, r_tile, width), lambda c, i: (c, i, 0))], carry)
    return out, got


def hidden_grad(cot, down_w, slope, r_tile, f_tile, carry, adds):
    rows, model = cot.shape
    ff = down_w.shape[0]
    grid = (ff // f_tile, rows // r_tile)
    extra_in, extra_out = side_sums(adds, grid)

    def inner(c_ref, w_ref, s_ref, *refs):
        sides, (g_ref, b_ref, *results) = refs[: len(extra_in)], refs[len(extra_in) :]
        for n in range(len(adds)):
            results[n][...] = add_low(sides[2 * n][...], sides[2 * n + 1][...])
        low = (dot_nt(c_ref[...], w_ref[...]) * s_ref[...].astype(f32)).astype(bf16)
        g_ref[...] = low
        part = jnp.sum(low.astype(f32).reshape(r_tile // 8, 8, f_tile), axis=0)

        @pl.when(pl.program_id(1) == 0)
        def _():
            b_ref[...] = part

        @pl.when(pl.program_id(1) > 0)
        def _():
            b_ref[...] += part

    (grad, sums, *results), got = tiled(
        inner, grid,
        [
            (cot, (r_tile, model), lambda j, i: (i, 0)),
            (down_w, (f_tile, model), lambda j, i: (j, 0)),
            (slope, (r_tile, f_tile), lambda j, i: (i, j)),
        ] + extra_in,
        [
            ((rows, ff), bf16, (r_tile, f_tile), lambda j, i: (i, j)),
            ((8, ff), f32, (8, f_tile), lambda j, i: (0, j)),
        ] + extra_out, carry)
    return grad, sums, results, got


def norm_gather(tokens, ln_gain, ln_bias, tag):
    local, model = tokens.shape
    half, tile = local // 2, local // 6

    def kernel(x_ref, gain_ref, bias_ref, all_ref, mine, sems):
        meet([("tensor", 1), ("tensor", 2)])
        part = lambda n: mine.at[pl.ds(n * half, half)]
        rows = lambda at, size: all_ref.at[pl.ds(at, size)]
        copies = remote_copies([
            (part(1), rows(local + half, half), "tensor", 1),
            (part(0), rows(2 * local, half), "tensor", 2),
            (part(0), rows(local, half), "tensor", 1),
            (part(1), rows(2 * local + half, half), "tensor", 2),
            (rows(2 * local, half), rows(3 * local, half), "tensor", 1),
            (rows(local + half, half), rows(3 * local + half, half), "tensor", 2),
            (mine, rows(0, local), None, 0),
        ], sems)

        def normalize(n):
            @pl.loop(0, 3)
            def _(i):
                at = pl.ds(pl.multiple_of(n * half + i * tile, tile), tile)
                xhat, inverse = norm_parts(x_ref[at, :].astype(f32))
                mine[at, :] = (xhat * gain_ref[...] + bias_ref[...]).astype(bf16)

        normalize(1)
        copies[0].start()
        normalize(0)
        for n in (1, 2, 3, 6):
            copies[n].start()
        copies[1].wait_recv()
        copies[4].start()
        copies[0].wait_recv()
        copies[5].start()
        copies[0].wait_send()
        copies[1].wait_send()
        for n in (2, 3, 4, 5, 6):
            copies[n].wait()

    return pl.pallas_call(
        kernel,
        in_specs=[pl.BlockSpec(memory_space=pltpu.VMEM)] * 3,
        out_specs=pl.BlockSpec(memory_space=pltpu.HBM),
        out_shape=jax.ShapeDtypeStruct((4 * local, model), bf16),
        scratch_shapes=[pltpu.VMEM((local, model), bf16), pltpu.SemaphoreType.DMA((2, 7))],
        compiler_params=pltpu.CompilerParams(
            vmem_limit_bytes=63 << 20, collective_id=tag, has_side_effects=True),
        cost_estimate=hint(),
    )(tokens, ln_gain[None], ln_bias[None])


def gather_sides(x, tag):
    local, model = x.shape
    return Carry(
        tag, [x], [((4 * local, model), bf16)],
        lambda src, dst: [
            (src[0], dst[0].at[pl.ds(local, local)], "tensor", 1),
            (src[0], dst[0].at[pl.ds(2 * local, local)], "tensor", 2),
            (src[0], dst[0].at[pl.ds(0, local)], None, 0),
        ], 3)


def gather_corner(whole, tag):
    local = whole.shape[0] // 4
    half = local // 2
    return Carry(
        tag, [whole], [(whole.shape, bf16)],
        lambda src, dst: [
            (dst[0].at[pl.ds(2 * local, half)], dst[0].at[pl.ds(3 * local, half)], "tensor", 1),
            (dst[0].at[pl.ds(local + half, half)], dst[0].at[pl.ds(3 * local + half, half)], "tensor", 2),
        ], 2, True)


def norm_back(own, low_parts, high_parts, tokens, cotangent, ln_gain):
    rows, model = tokens.shape
    tiles = 6
    tile = rows // tiles
    half = tiles // 2

    def inner(own_low, own_high, l0, l1, h0, h1, t_ref, c_ref, gain_ref, o_ref, s_ref):
        step = pl.program_id(0)

        def compute(a, b, c):
            grad = a[...].astype(f32) + b[...].astype(f32) + c[...].astype(f32)
            cot = c_ref[...].astype(f32)
            xhat, inverse = norm_parts(t_ref[...].astype(f32))
            scaled = grad * gain_ref[...]
            both = grad * xhat
            o_ref[...] = cot + inverse * (
                scaled
                - jnp.mean(scaled, axis=-1, keepdims=True)
                - xhat * jnp.mean(scaled * xhat, axis=-1, keepdims=True))
            terms = [jnp.sum(v.reshape(tile // 8, 8, model), axis=0) for v in (both, grad, cot)]

            @pl.when(step == 0)
            def _():
                for n in range(3):
                    s_ref[n] = terms[n]

            @pl.when(step > 0)
            def _():
                for n in range(3):
                    s_ref[n] += terms[n]

        @pl.when(step < half)
        def _():
            compute(own_low, l0, l1)

        @pl.when(step >= half)
        def _():
            compute(own_high, h0, h1)

    low = lambda i: (jnp.minimum(i, half - 1), 0)
    high = lambda i: (jnp.maximum(i - half, 0), 0)
    each = lambda i: (i, 0)
    block = (tile, model)
    (grad, sums), ignored = tiled(
        inner, (tiles,),
        [(own[0], block, low), (own[1], block, high)]
        + [(a, block, low) for a in low_parts] + [(a, block, high) for a in high_parts]
        + [(tokens, block, each), (cotangent, block, each), (ln_gain[None], (1, model), lambda i: (0, 0))],
        [((rows, model), f32, block, each), ((3, 8, model), f32, (3, 8, model), lambda i: (0, 0, 0))])
    return grad, jnp.sum(sums, axis=1)


def norm_parts(rows_in):
    row_mean = jnp.mean(rows_in, axis=-1, keepdims=True)
    centred = rows_in - row_mean
    inverse = lax.rsqrt(jnp.mean(centred * centred, axis=-1, keepdims=True) + norm_eps)
    return centred * inverse, inverse


def gelu_parts(v):
    scale = (2.0 / jnp.pi) ** 0.5
    square = v * v
    t = jnp.tanh(v * (scale + (scale * 0.044715) * square))
    half = 0.5 * (1.0 + t)
    slope = half + (half * (1.0 - t)) * (v * (scale + (scale * 3 * 0.044715) * square))
    return v * half, slope


def body(
    tokens,
    cotangent,
    ln_gain,
    ln_bias,
    w_qkv,
    b_qkv,
    w_out,
    w_fc1,
    b_fc1,
    w_fc2,
    resid_bias,
    parents,
):
    size = lax.axis_size("tensor")
    groups = lax.axis_size("dp")
    local_rows, model = tokens.shape
    me = lax.axis_index("tensor")
    width = w_qkv.shape[2]
    four = size == 4
    t1, t2 = ("tensor", 1), ("tensor", 2)
    half_cols = model // 2

    tables = rope_tables()
    up_w = lax.all_gather(w_fc1, "dp", axis=0, tiled=True)
    qkv_w = lax.all_gather(w_qkv, "dp", axis=1, tiled=True)
    out_w = lax.all_gather(w_out, "dp", axis=1, tiled=True)
    down_w = lax.all_gather(w_fc2, "dp", axis=1, tiled=True)
    if four:
        normed = norm_gather(tokens, ln_gain, ln_bias, 1)
    else:
        normed_local = (norm_parts(tokens.astype(f32))[0] * ln_gain + ln_bias).astype(bf16)
        normed, cot_full = (
            jnp.concatenate([x] + [xor_send(x, i, size) for i in range(1, size)], axis=0)
            for x in (normed_local, cotangent))
    activated, slope, got = hidden_forward(
        normed, up_w, b_fc1, local_rows, half_cols, gather_sides(cotangent, 2) if four else None)
    projected, got = project(
        after(normed, activated), qkv_w, b_qkv, local_rows, gather_corner(got[0], 3) if four else None)
    if four:
        cot_full = got[0]
    grad_w_fc2 = dot_tn(after(activated, projected), cot_full).astype(bf16)
    summed_fc2 = lax.psum_scatter(grad_w_fc2, "dp", scatter_dimension=1, tiled=True)
    grad_attended = dot_nt(after(cot_full, grad_w_fc2), out_w).astype(bf16)
    attended, grad_qkv, aux = attention(parents[0], me[None], size, *tables, projected, grad_attended)

    grad_w_out = dot_tn(attended, cot_full).astype(bf16)
    summed_out = lax.psum_scatter(grad_w_out, "dp", scatter_dimension=1, tiled=True)
    branch, ignored = chunk_matmul(
        [(after(attended, grad_w_out), out_w, -1, None), (activated, down_w, -1, None)],
        model, half_cols, size, size, lambda i: i, cut=2)
    grad_w_qkv, got = qkv_grads(
        after(normed, branch[0]), grad_qkv, half_cols,
        sending(4, (branch[6],) + t1, (branch[7],) + t2) if four else None)
    summed_qkv = lax.psum_scatter(grad_w_qkv, "dp", scatter_dimension=1, tiled=True)
    grad_hidden, sums_fc1, branch_next, side = hidden_grad(
        after(cot_full, grad_w_qkv), down_w, slope, local_rows, half_cols,
        sending(5, (branch[2],) + t1, (branch[5],) + t2) if four else None,
        [(branch[3], got[1]), (branch[4], got[0])] if four else [])
    dp_bits = range(1, groups)
    backs = [(grad_qkv, qkv_w, c, c) for c in range(3)] + [(after(grad_hidden, summed_fc2), up_w, -1, -1)]
    if four:
        far, last = chunk_matmul(
            backs, model, half_cols, 8, 4, lambda i: 7 - i - 2 * (i // 3),
            sending(6, (branch_next[0],) + t1, (branch_next[1],) + t2))
        branch_sum = [
            branch[0].astype(f32) + side[0].astype(f32) + last[1].astype(f32),
            branch[1].astype(f32) + last[0].astype(f32) + side[1].astype(f32)]
        grad_w_fc1, got = weight_grad(
            after(normed, far[7], summed_out), grad_hidden, half_cols, half_cols,
            sending(
                7, (far[6],) + t1, (far[7],) + t2,
                *[(aux, "dp", bits) for bits in dp_bits], *[(sums_fc1, "dp", bits) for bits in dp_bits]))
        all_aux = [aux] + got[2 : 1 + groups]
        all_fc1 = [sums_fc1] + got[1 + groups :]
        backs[3] = (after(grad_hidden, grad_w_fc1),) + backs[3][1:]
        near, side = chunk_matmul(
            backs, model, half_cols, 8, 4, lambda i: 4 - i - i // 2,
            sending(8, (far[2],) + t1, (far[5],) + t2), {3: got[1], 4: got[0]})
        one, two = xor_send(near[3], 1, size), xor_send(near[4], 2, size)
        input_grad, terms = norm_back(
            [near[0], near[1]], [side[0], two], [one, side[1]], tokens, cotangent, ln_gain)
        branch_sum[0] = after(branch_sum[0], near[0])
        all_aux[0] = after(aux, near[0])
        all_fc1[0] = after(sums_fc1, near[0])
        summed_qkv, summed_out, summed_fc2 = lax.optimization_barrier((summed_qkv, summed_out, summed_fc2, near[0]))[:3]
    else:
        parts, ignored = chunk_matmul(backs, model, half_cols, size, size, lambda i: i, cut=2)
        grad_w_fc1, ignored = weight_grad(normed, grad_hidden, half_cols, half_cols, None)
        all_aux, all_fc1 = (list(lax.all_gather(x, "dp")) for x in (aux, sums_fc1))
        branch_sum = scatter_rest(branch, size)
        grad_normed = jnp.concatenate(scatter_rest(parts, size), axis=0)
        xhat, inverse = norm_parts(tokens.astype(f32))
        grad_xhat = grad_normed * ln_gain
        cot_local = cotangent.astype(f32)
        input_grad = cot_local + inverse * (
            grad_xhat
            - jnp.mean(grad_xhat, axis=-1, keepdims=True)
            - xhat * jnp.mean(grad_xhat * xhat, axis=-1, keepdims=True)
        )
        terms = jnp.stack(
            [jnp.sum(grad_normed * xhat, axis=0), jnp.sum(grad_normed, axis=0), jnp.sum(cot_local, axis=0)]
        )
    summed_fc1 = lax.psum_scatter(grad_w_fc1, "dp", scatter_dimension=0, tiled=True)
    output_rows = (
        tokens.astype(f32) + jnp.concatenate(branch_sum, axis=0) + resid_bias).astype(bf16)
    summed_fc1, summed_qkv, summed_out, summed_fc2 = (
        w.astype(f32) for w in (summed_fc1, summed_qkv, summed_out, summed_fc2))

    bias_qkv = jnp.transpose(sum(a[:, :3] for a in all_aux), (1, 0, 2)).reshape(3, width)
    bias_fc1 = jnp.sum(sum(all_fc1), axis=0)
    head_top = functools.reduce(jnp.maximum, [a[:, 3:5, 0] for a in all_aux]).reshape(-1)
    factor = jnp.sqrt(clip_tau / jnp.maximum(head_top, clip_tau))
    clipped_qk = (w_qkv[:2].astype(f32) * jnp.repeat(factor, HDIM)[None, None, :]).astype(bf16)

    every = size * groups
    pieces = jnp.transpose(terms.reshape(3, every, model // every), (1, 0, 2)).reshape(every, -1)
    pieces = lax.all_to_all(pieces, ("dp", "tensor"), 0, 0, tiled=True)
    grad_small = jnp.sum(pieces, axis=0).reshape(3, model // every)
    return (
        output_rows,
        input_grad,
        grad_small,
        summed_qkv,
        bias_qkv,
        summed_out,
        summed_fc1,
        bias_fc1,
        summed_fc2,
        clipped_qk,
    )


def solution(mesh):
    return jax.shard_map(
        body,
        mesh=mesh,
        in_specs=(
            P(("dp", "tensor"), None),
            P(("dp", "tensor"), None),
            P(),
            P(),
            P(None, "dp", "tensor"),
            P(None, "tensor"),
            P("tensor", "dp"),
            P("dp", "tensor"),
            P("tensor"),
            P("tensor", "dp"),
            P(),
            P("dp", None),
        ),
        out_specs=(
            P(("dp", "tensor"), None),
            P(("dp", "tensor"), None),
            P(None, ("dp", "tensor")),
            P(None, "dp", "tensor"),
            P(None, "tensor"),
            P("tensor", "dp"),
            P("dp", "tensor"),
            P("tensor"),
            P("tensor", "dp"),
            P(None, "dp", "tensor"),
        ),
        check_vma=False,
    )
```

```python
import functools

import jax
import jax.numpy as jnp
import numpy as np
from jax import lax
from jax.experimental import pallas as pl
from jax.experimental.pallas import tpu as pltpu
from jax.sharding import PartitionSpec as P

HDIM = 64
ROT = 32
SEG = 128
TRUNK = 6
BRANCHES = 4
LEAVES = 2
TREE_SEGS = TRUNK + BRANCHES + BRANCHES * LEAVES
bf16 = jnp.bfloat16
f32 = jnp.float32
NEG = -1e30
rope_base = 10000.0


def dot_nn(a, b):
    return lax.dot_general(a, b, (((1,), (0,)), ((), ())), preferred_element_type=f32)


def dot_nt(a, b):
    return lax.dot_general(a, b, (((1,), (1,)), ((), ())), preferred_element_type=f32)


def rope_tables():
    lane = np.arange(2 * HDIM) % HDIM
    freq = np.where(lane < ROT, rope_base ** (-2.0 * (lane % (ROT // 2)) / ROT), 0.0)
    angles = np.concatenate([np.arange(SEG), SEG * np.arange(TRUNK + 2)])[:, None] * freq[None, :]
    return np.cos(angles).astype(np.float32), np.sin(angles).astype(np.float32)


def partner(x):
    lane = lax.broadcasted_iota(jnp.int32, x.shape, 1) % HDIM
    half = ROT // 2
    return jnp.where(lane < half, pltpu.roll(x, 2 * HDIM - half, 1), pltpu.roll(x, half, 1))


def attn_kernel(size, par, me, cos_in, sin_in, qkv_ref, do_in, att_ref, g_ref, aux_ref,
                qs, kr, vr, do_ref, kt, vt, dot_t, att, dqn, dk, dv, s_ref, top, cos_ref, sin_ref):
    rows = TREE_SEGS * SEG
    step = 2 * SEG
    local = rows // size
    lane_low = lax.broadcasted_iota(jnp.int32, (step, 2 * HDIM), 1) < HDIM

    def unit(n):
        return jnp.where(
            lax.broadcasted_iota(jnp.int32, (n, n), 0) == lax.broadcasted_iota(jnp.int32, (n, n), 1),
            1.0, 0.0).astype(bf16)

    unit_wide = unit(2 * HDIM)

    def places(i):
        here = pl.ds(i * local, local)
        there = pl.ds(pl.multiple_of((me[0] ^ i) * local, local), local)
        return here, there

    @pl.when(pl.program_id(0) == 0)
    def _():
        sign = jnp.where(lax.broadcasted_iota(jnp.int32, (SEG, 2 * HDIM), 1) % HDIM < ROT // 2, -1.0, 1.0)
        cos_place, sin_place = cos_in[:SEG, :], sin_in[:SEG, :]
        for depth in range(TRUNK + 2):
            cos_seg, sin_seg = cos_in[SEG + depth : SEG + depth + 1, :], sin_in[SEG + depth : SEG + depth + 1, :]
            cos = cos_place * cos_seg - sin_place * sin_seg
            sin = (sin_place * cos_seg + cos_place * sin_seg) * sign
            first = [depth] if depth < TRUNK else range(TRUNK, TRUNK + BRANCHES)
            for seg in first if depth <= TRUNK else range(TRUNK + BRANCHES, TREE_SEGS):
                cos_ref[seg * SEG : (seg + 1) * SEG, :] = cos
                sin_ref[seg * SEG : (seg + 1) * SEG, :] = sin

    for i in range(size):
        here, there = places(i)
        cos, sin = cos_ref[there, :], sin_ref[there, :]
        q = qkv_ref[0, here, :].astype(f32)
        k = qkv_ref[1, here, :].astype(f32)
        qs[there, :] = ((q * cos + partner(q) * sin) * (HDIM ** -0.5)).astype(bf16)
        kr[there, :] = (k * cos + partner(k) * sin).astype(bf16)
        vr[there, :] = qkv_ref[2, here, :]
        do_ref[there, :] = do_in[here, :]

    for i in range(rows // step):
        at = pl.ds(i * step, step)
        kt[:, at] = dot_nt(unit_wide, kr[at, :]).astype(bf16)
        vt[:, at] = dot_nt(unit_wide, vr[at, :]).astype(bf16)
        dot_t[:, at] = dot_nt(unit_wide, do_ref[at, :]).astype(bf16)
        dk[at, :] = jnp.zeros((step, 2 * HDIM), f32)
        dv[at, :] = jnp.zeros((step, 2 * HDIM), f32)

    top[...] = jnp.full((2, 8, step), NEG, f32)
    key_id = lax.broadcasted_iota(jnp.int32, (SEG, step), 0)
    query_id = lax.broadcasted_iota(jnp.int32, (SEG, step), 1) % SEG
    pair_mask = key_id <= query_id
    tri_mask = lax.broadcasted_iota(jnp.int32, (step, step), 0) <= lax.broadcasted_iota(
        jnp.int32, (step, step), 1)

    def seg_at(start, size):
        if isinstance(start, int):
            return pl.ds(start, size)
        return pl.ds(pl.multiple_of(start, SEG), size)

    def block(q0, q1, chunks, diag):
        halves = [seg_at(q0, SEG), seg_at(q1, SEG)]
        q_all = jnp.concatenate([qs[halves[0], :], qs[halves[1], :]], axis=0)
        do_all = jnp.concatenate([do_ref[halves[0], :], do_ref[halves[1], :]], axis=0)
        zero = jnp.zeros_like(q_all)
        pieces = []
        off = 0
        for start, size in chunks:
            pieces.append((off, start, size, 'full'))
            off += size
        pieces.append((off, q0, step, 'tri') if diag else (off, None, SEG, 'pair'))
        both = range(2)
        qh = [jnp.where(lane_low if h == 0 else ~lane_low, q_all, zero) for h in both]
        dh = [jnp.where(lane_low if h == 0 else ~lane_low, do_all, zero) for h in both]
        q_stack = jnp.concatenate(qh, axis=0)
        d_stack = jnp.concatenate(dh, axis=0)

        def part(x, i):
            return x[i * SEG:(i + 1) * SEG]

        def lanes(x, i):
            return x[:, i * SEG:(i + 1) * SEG]

        def left(ref, piece, stack):
            o, start, size, kind = piece
            if kind == 'pair':
                each = [
                    dot_nt(ref[halves[i], :], jnp.concatenate([part(stack, i), part(stack, 2 + i)], axis=0))
                    for i in both]
                return [jnp.concatenate([lanes(x, h) for x in each], axis=1) for h in both]
            x = dot_nt(ref[seg_at(start, size), :], stack)
            return [x[:, h * step : (h + 1) * step] for h in both]

        def turned(ref, h, piece, x):
            o, start, size, kind = piece
            rows_h = slice(h * HDIM, (h + 1) * HDIM)
            if kind == 'pair':
                return jnp.concatenate(
                    [dot_nn(ref[rows_h, halves[i]], lanes(x, i)) for i in both], axis=1)
            return dot_nn(ref[rows_h, seg_at(start, size)], x)

        def add_rows(ref, piece, xs, stack):
            o, start, size, kind = piece
            if kind == 'pair':
                for i in both:
                    ref[halves[i], :] += dot_nn(
                        jnp.concatenate([lanes(x, i) for x in xs], axis=1),
                        jnp.concatenate([part(stack, i), part(stack, 2 + i)], axis=0))
            else:
                ref[seg_at(start, size), :] += dot_nn(jnp.concatenate(xs, axis=1), stack)

        def fold(x, op):
            return op(x.reshape(x.shape[0] // 8, 8, step), axis=0)

        tops = [[], []]
        sums = [[], []]
        for piece in pieces:
            o, start, size, kind = piece
            scores = left(kr, piece, q_stack)
            for h in both:
                s = scores[h]
                if kind == 'tri':
                    s = jnp.where(tri_mask, s, NEG)
                if kind == 'pair':
                    s = jnp.where(pair_mask, s, NEG)
                m = fold(s, jnp.max)
                top[h] = jnp.maximum(top[h], m)
                m = jnp.max(m, axis=0, keepdims=True)
                e = jnp.exp(s - m)
                s_ref[h, o:o + size, :] = e
                tops[h].append(m)
                sums[h].append(jnp.sum(fold(e, jnp.sum), axis=0, keepdims=True))
        scales = []
        for h in both:
            m = functools.reduce(jnp.maximum, tops[h])
            w = [jnp.exp(mc - m) for mc in tops[h]]
            inv = 1.0 / sum(wc * sc for wc, sc in zip(w, sums[h]))
            scales.append([wc * inv for wc in w])
        o_acc = [jnp.zeros((HDIM, step), f32)] * 2
        for n, piece in enumerate(pieces):
            o, start, size, kind = piece
            low = []
            for h in both:
                p = s_ref[h, o:o + size, :] * scales[h][n]
                s_ref[h, o:o + size, :] = p
                low.append(p.astype(bf16))
                o_acc[h] = o_acc[h] + turned(vt, h, piece, low[h])
            add_rows(dv, piece, low, d_stack)
        deltas = []
        for h in both:
            d_turned = jnp.concatenate(
                [dot_t[h * HDIM:(h + 1) * HDIM, halves[i]] for i in both], axis=1)
            deltas.append(jnp.sum(o_acc[h] * d_turned.astype(f32), axis=0, keepdims=True))
        dq_acc = [jnp.zeros((HDIM, step), f32)] * 2
        for n, piece in enumerate(pieces):
            o, start, size, kind = piece
            low = []
            dps = left(vr, piece, d_stack)
            for h in both:
                low.append((s_ref[h, o:o + size, :] * (dps[h] - deltas[h])).astype(bf16))
                dq_acc[h] = dq_acc[h] + turned(kt, h, piece, low[h])
            add_rows(dk, piece, low, q_stack)
        o_rows = jnp.concatenate(o_acc, axis=0).T.astype(bf16)
        dq_rows = jnp.concatenate(dq_acc, axis=0).T
        for i in both:
            att[halves[i], :] = part(o_rows, i)
            dqn[halves[i], :] = part(dq_rows, i)

    for b in range(TRUNK // 2):
        block(b * step, b * step + SEG, [(c * step, step) for c in range(b)], True)
    trunk_chunks = [(c * step, step) for c in range(TRUNK // 2)]

    @pl.loop(0, BRANCHES // 2)
    def _(i):
        start = (TRUNK + 2 * i) * SEG
        block(start, start + SEG, trunk_chunks, False)

    @pl.loop(0, BRANCHES)
    def _(i):
        branch = TRUNK + i
        first = TREE_SEGS - 1
        last = TRUNK + BRANCHES
        for leaf in range(TREE_SEGS - 1, TRUNK + BRANCHES - 1, -1):
            first = jnp.where(par[leaf] == branch, leaf, first)
        for leaf in range(TRUNK + BRANCHES, TREE_SEGS):
            last = jnp.where(par[leaf] == branch, leaf, last)
        block(first * SEG, last * SEG, trunk_chunks + [(branch * SEG, SEG)], False)

    totals = [jnp.zeros((8, 2 * HDIM), f32)] * 3
    for i in range(size):
        here, there = places(i)
        cos, sin = cos_ref[there, :], sin_ref[there, :]
        att_ref[here, :] = att[there, :]
        dq = dqn[there, :] * (HDIM ** -0.5)
        dkr = dk[there, :]
        parts = [dq * cos - partner(dq) * sin, dkr * cos - partner(dkr) * sin, dv[there, :]]
        for c in range(3):
            low = parts[c].astype(bf16)
            g_ref[c, here, :] = low
            totals[c] = totals[c] + jnp.sum(low.astype(f32).reshape(local // 8, 8, 2 * HDIM), axis=0)

    rows_out = [jnp.sum(t, axis=0, keepdims=True) for t in totals]
    for h in range(2):
        rows_out.append(jnp.full((1, 2 * HDIM), jnp.max(top[h]), f32))
    rows_out.append(jnp.zeros((3, 2 * HDIM), f32))
    aux_ref[0] = jnp.concatenate(rows_out, axis=0)


def attention(parents, me, size, cos, sin, qkv, grad_att):
    rows, width = grad_att.shape
    pairs = width // (2 * HDIM)
    step = 2 * SEG
    wide = 2 * HDIM
    keys = TRUNK * SEG + 2 * SEG
    blk = lambda: pl.BlockSpec((rows, wide), lambda p, par, me: (0, p))
    blk3 = lambda: pl.BlockSpec((3, rows, wide), lambda p, par, me: (0, 0, p))
    tab = lambda: pl.BlockSpec((SEG + TRUNK + 2, wide), lambda p, par, me: (0, 0))
    return pl.pallas_call(
        functools.partial(attn_kernel, size),
        out_shape=(
            jax.ShapeDtypeStruct((rows, width), bf16),
            jax.ShapeDtypeStruct((3, rows, width), bf16),
            jax.ShapeDtypeStruct((pairs, 8, wide), f32),
        ),
        grid_spec=pltpu.PrefetchScalarGridSpec(
            num_scalar_prefetch=2,
            grid=(pairs,),
            in_specs=[tab(), tab(), blk3(), blk()],
            out_specs=[blk(), blk3(), pl.BlockSpec((1, 8, wide), lambda p, par, me: (p, 0, 0))],
            scratch_shapes=[
                pltpu.VMEM((rows, wide), bf16),
                pltpu.VMEM((rows, wide), bf16),
                pltpu.VMEM((rows, wide), bf16),
                pltpu.VMEM((rows, wide), bf16),
                pltpu.VMEM((wide, rows), bf16),
                pltpu.VMEM((wide, rows), bf16),
                pltpu.VMEM((wide, rows), bf16),
                pltpu.VMEM((rows, wide), bf16),
                pltpu.VMEM((rows, wide), f32),
                pltpu.VMEM((rows, wide), f32),
                pltpu.VMEM((rows, wide), f32),
                pltpu.VMEM((2, keys, step), f32),
                pltpu.VMEM((2, 8, step), f32),
                pltpu.VMEM((rows, wide), f32),
                pltpu.VMEM((rows, wide), f32),
            ],
        ),
        compiler_params=pltpu.CompilerParams(
            dimension_semantics=("arbitrary",), vmem_limit_bytes=63 << 20),
        cost_estimate=pl.CostEstimate(flops=60 * 10**9, transcendentals=17 * 10**6, bytes_accessed=24 << 20),
    )(parents, me, cos, sin, qkv, grad_att)


clip_tau = 10.0
norm_eps = 1e-05


def dot_tn(a, b):
    return lax.dot_general(a, b, (((0,), (0,)), ((), ())), preferred_element_type=f32)


def xor_send(x, bits, size):
    return lax.ppermute(x, "tensor", [(i, i ^ bits) for i in range(size)])


def add_low(a, b):
    return (a.astype(f32) + b.astype(f32)).astype(bf16)


def scatter_rest(parts, size):
    low, high = parts[0].astype(f32), parts[1].astype(f32)
    for i in range(1, size):
        low = low + xor_send(parts[2 * i], i, size).astype(f32)
        high = high + xor_send(parts[2 * i + 1], i, size).astype(f32)
    return [low, high]


def after(x, *others):
    return lax.optimization_barrier((x,) + others)[0]


class Carry:
    def __init__(self, tag=0, arrays=(), shapes=(), links=None, count=0, alias=False):
        self.tag, self.arrays, self.links, self.count, self.alias = tag, list(arrays), links, count, alias
        self.shapes = [jax.ShapeDtypeStruct(*shape) for shape in shapes]


def sending(tag, *sends):
    return Carry(
        tag, [a for a, axis, bits in sends], [(a.shape, a.dtype) for a, axis, bits in sends],
        lambda src, dst: [(src[n], dst[n], axis, bits) for n, (a, axis, bits) in enumerate(sends)], len(sends))


def other_device(axis, bits):
    t = lax.axis_index(axis)
    at = t
    for n in range(8):
        if bits >> n & 1:
            at = at + (1 << n) - (2 << n) * ((t // (1 << n)) % 2)
    return {axis: at}


def meet(partners):
    barrier = pltpu.get_barrier_semaphore()
    for axis, bits in partners:
        pl.semaphore_signal(
            barrier, inc=1, device_id=other_device(axis, bits), device_id_type=pl.DeviceIdType.MESH)
    pl.semaphore_wait(barrier, len(partners))


def remote_copies(links, sems):
    return [
        pltpu.make_async_copy(src, dst, sems.at[0, n])
        if axis is None
        else pltpu.make_async_remote_copy(
            src_ref=src,
            dst_ref=dst,
            send_sem=sems.at[0, n],
            recv_sem=sems.at[1, n],
            device_id=other_device(axis, bits),
            device_id_type=pl.DeviceIdType.MESH,
        )
        for n, (src, dst, axis, bits) in enumerate(links)
    ]


def hint():
    return pl.CostEstimate(flops=10**10, transcendentals=0, bytes_accessed=2 << 20)


def tiled(inner, grid, ins, outs, carry=None, vmem=63):
    carry = carry or Carry()
    n_in, n_out, n_src, n_dst = len(ins), len(outs), len(carry.arrays), len(carry.shapes)
    in_specs = [pl.BlockSpec(block, at) for a, block, at in ins]
    out_specs = [pl.BlockSpec(block, at) for shape, dtype, block, at in outs]
    any_spec = pl.BlockSpec(memory_space=pltpu.HBM)
    arrays = [a for a, block, at in ins]
    shapes = [jax.ShapeDtypeStruct(shape, dtype) for shape, dtype, block, at in outs]
    if not carry.count:
        results = pl.pallas_call(
            inner, grid=grid, in_specs=in_specs, out_specs=out_specs, out_shape=shapes,
            compiler_params=pltpu.CompilerParams(
                dimension_semantics=("arbitrary",) * len(grid), vmem_limit_bytes=vmem << 20),
            cost_estimate=hint(),
        )(*arrays)
        return list(results), []

    def kernel(*refs):
        sources = refs[n_in : n_in + n_src]
        places = refs[n_in + n_src : n_in + n_src + n_out]
        targets = refs[n_in + n_src + n_out : -1]
        links = carry.links(sources, targets)
        meet(sorted(set((axis, bits) for src, dst, axis, bits in links if axis is not None)))
        copies = remote_copies(links, refs[-1])
        for copy in copies:
            copy.start()
        if grid:
            pltpu.emit_pipeline(inner, grid=grid, in_specs=in_specs, out_specs=out_specs)(*refs[:n_in], *places)
        for copy in copies:
            copy.wait()

    results = pl.pallas_call(
        kernel,
        in_specs=[any_spec] * (n_in + n_src),
        out_specs=[any_spec] * (n_out + n_dst),
        out_shape=shapes + carry.shapes,
        scratch_shapes=[pltpu.SemaphoreType.DMA((2, carry.count))],
        input_output_aliases={n_in: n_out} if carry.alias else {},
        compiler_params=pltpu.CompilerParams(
            vmem_limit_bytes=vmem << 20, collective_id=carry.tag, has_side_effects=True),
        cost_estimate=hint(),
    )(*arrays, *carry.arrays)
    return list(results[:n_out]), list(results[n_out:])


def side_sums(adds, grid):
    at = lambda j, i: (0, j * grid[1] + i)
    block = lambda a: (a.shape[0], a.shape[1] // (grid[0] * grid[1]))
    ins = [(a, block(a), at) for pair in adds for a in pair]
    outs = [(a.shape, a.dtype, block(a), at) for a, b in adds]
    return ins, outs


def chunk_matmul(pairs, columns, tile, count, blocks, at, carry=None, adds=(), cut=1):
    local = pairs[0][0].shape[-2] // count
    grid = (columns // tile, blocks)
    ins = []
    for x, w, c, d in pairs:
        depth = x.shape[-1]
        if c < 0:
            ins.append((x, (local, depth), lambda j, i: (at(i), 0)))
        else:
            ins.append((x, (None, local, depth), lambda j, i, c=c: (c, at(i), 0)))
        if d is None:
            ins.append((w, (depth, tile), lambda j, i: (0, j)))
        elif d < 0:
            ins.append((w, (tile, depth), lambda j, i: (j, 0)))
        else:
            ins.append((w, (None, tile, depth), lambda j, i, d=d: (d, j, 0)))
    terms = len(pairs)
    adds = dict(adds)
    more = [(adds[b], (local, tile), lambda j, i: (0, j)) for b in sorted(adds)]
    part = local // cut
    outs = [((part, columns), bf16, (part, tile), lambda j, i: (0, j))] * (blocks * cut)

    def inner(*refs):
        sides, results = dict(zip(sorted(adds), refs[2 * terms :])), refs[2 * terms + len(more) :]
        acc = None
        for n in range(terms):
            dot = dot_nn if pairs[n][3] is None else dot_nt
            term = dot(refs[2 * n][...], refs[2 * n + 1][...])
            acc = term if acc is None else acc + term
        for i in range(blocks):
            @pl.when(pl.program_id(1) == i)
            def _(i=i):
                whole = acc
                if at(i) in sides:
                    whole = whole + sides[at(i)][...].astype(f32)
                low = whole.astype(bf16)
                for n in range(cut):
                    results[i * cut + n][...] = low[n * part : (n + 1) * part]

    results, got = tiled(inner, grid, ins + more, outs, carry)
    return {at(i) * cut + n: results[i * cut + n] for i in range(blocks) for n in range(cut)}, got


def qkv_grads(normed, grad_qkv, tile, carry):
    rows, model = normed.shape
    width = grad_qkv.shape[2]

    def inner(n_ref, g_ref, o_ref):
        o_ref[...] = dot_tn(n_ref[...], g_ref[...]).astype(bf16)

    (grads,), got = tiled(
        inner, (3, model // tile),
        [
            (normed, (rows, tile), lambda c, i: (0, i)),
            (grad_qkv, (None, rows, width), lambda c, i: (c, 0, 0)),
        ],
        [((3, model, width), bf16, (None, tile, width), lambda c, i: (c, i, 0))], carry)
    return grads, got


def weight_grad(x, y, m_tile, n_tile, carry):
    rows, m = x.shape
    n = y.shape[1]

    def inner(x_ref, y_ref, o_ref):
        o_ref[...] = dot_tn(x_ref[...], y_ref[...]).astype(bf16)

    (grad,), got = tiled(
        inner, (m // m_tile, n // n_tile),
        [(x, (rows, m_tile), lambda i, j: (0, i)), (y, (rows, n_tile), lambda i, j: (0, j))],
        [((m, n), bf16, (m_tile, n_tile), lambda i, j: (i, j))], carry)
    return grad, got


def hidden_forward(normed, up_w, b_fc1, r_tile, f_tile, carry):
    rows, model = normed.shape
    ff = up_w.shape[1]

    def inner(n_ref, w_ref, b_ref, a_ref, s_ref):
        value, slope = gelu_parts(dot_nn(n_ref[...], w_ref[...]) + b_ref[...])
        a_ref[...] = value.astype(bf16)
        s_ref[...] = slope.astype(bf16)

    out = ((rows, ff), bf16, (r_tile, f_tile), lambda j, i: (i, j))
    (value, slope), got = tiled(
        inner, (ff // f_tile, rows // r_tile),
        [
            (normed, (r_tile, model), lambda j, i: (i, 0)),
            (up_w, (model, f_tile), lambda j, i: (0, j)),
            (b_fc1[None], (1, f_tile), lambda j, i: (0, j)),
        ],
        [out, out], carry, 48)
    return value, slope, got


def hidden_grad(cot, down_w, slope, r_tile, f_tile, carry, adds):
    rows, model = cot.shape
    ff = down_w.shape[0]
    grid = (ff // f_tile, rows // r_tile)
    extra_in, extra_out = side_sums(adds, grid)

    def inner(c_ref, w_ref, s_ref, *refs):
        sides, (g_ref, b_ref, *results) = refs[: len(extra_in)], refs[len(extra_in) :]
        for n in range(len(adds)):
            results[n][...] = add_low(sides[2 * n][...], sides[2 * n + 1][...])
        low = (dot_nt(c_ref[...], w_ref[...]) * s_ref[...].astype(f32)).astype(bf16)
        g_ref[...] = low
        part = jnp.sum(low.astype(f32).reshape(r_tile // 8, 8, f_tile), axis=0)

        @pl.when(pl.program_id(1) == 0)
        def _():
            b_ref[...] = part

        @pl.when(pl.program_id(1) > 0)
        def _():
            b_ref[...] += part

    (grad, sums, *results), got = tiled(
        inner, grid,
        [
            (cot, (r_tile, model), lambda j, i: (i, 0)),
            (down_w, (f_tile, model), lambda j, i: (j, 0)),
            (slope, (r_tile, f_tile), lambda j, i: (i, j)),
        ] + extra_in,
        [
            ((rows, ff), bf16, (r_tile, f_tile), lambda j, i: (i, j)),
            ((8, ff), f32, (8, f_tile), lambda j, i: (0, j)),
        ] + extra_out, carry)
    return grad, sums, results, got


def norm_gather(tokens, ln_gain, ln_bias, tag):
    local, model = tokens.shape
    half, tile = local // 2, local // 6

    def kernel(x_ref, gain_ref, bias_ref, all_ref, mine, sems):
        meet([("tensor", 1), ("tensor", 2)])
        part = lambda n: mine.at[pl.ds(n * half, half)]
        rows = lambda at, size: all_ref.at[pl.ds(at, size)]
        copies = remote_copies([
            (part(1), rows(local + half, half), "tensor", 1),
            (part(0), rows(2 * local, half), "tensor", 2),
            (part(0), rows(local, half), "tensor", 1),
            (part(1), rows(2 * local + half, half), "tensor", 2),
            (rows(2 * local, half), rows(3 * local, half), "tensor", 1),
            (rows(local + half, half), rows(3 * local + half, half), "tensor", 2),
            (mine, rows(0, local), None, 0),
        ], sems)

        def normalize(n):
            @pl.loop(0, 3)
            def _(i):
                at = pl.ds(pl.multiple_of(n * half + i * tile, tile), tile)
                xhat, inverse = norm_parts(x_ref[at, :].astype(f32))
                mine[at, :] = (xhat * gain_ref[...] + bias_ref[...]).astype(bf16)

        normalize(1)
        copies[0].start()
        normalize(0)
        for n in (1, 2, 3, 6):
            copies[n].start()
        copies[1].wait_recv()
        copies[4].start()
        copies[0].wait_recv()
        copies[5].start()
        copies[0].wait_send()
        copies[1].wait_send()
        for n in (2, 3, 4, 5, 6):
            copies[n].wait()

    return pl.pallas_call(
        kernel,
        in_specs=[pl.BlockSpec(memory_space=pltpu.VMEM)] * 3,
        out_specs=pl.BlockSpec(memory_space=pltpu.HBM),
        out_shape=jax.ShapeDtypeStruct((4 * local, model), bf16),
        scratch_shapes=[pltpu.VMEM((local, model), bf16), pltpu.SemaphoreType.DMA((2, 7))],
        compiler_params=pltpu.CompilerParams(
            vmem_limit_bytes=63 << 20, collective_id=tag, has_side_effects=True),
        cost_estimate=hint(),
    )(tokens, ln_gain[None], ln_bias[None])


def gather_sides(x, tag):
    local, model = x.shape
    return Carry(
        tag, [x], [((4 * local, model), bf16)],
        lambda src, dst: [
            (src[0], dst[0].at[pl.ds(local, local)], "tensor", 1),
            (src[0], dst[0].at[pl.ds(2 * local, local)], "tensor", 2),
            (src[0], dst[0].at[pl.ds(0, local)], None, 0),
        ], 3)


def gather_corner(whole, tag):
    local = whole.shape[0] // 4
    half = local // 2
    return Carry(
        tag, [whole], [(whole.shape, bf16)],
        lambda src, dst: [
            (dst[0].at[pl.ds(2 * local, half)], dst[0].at[pl.ds(3 * local, half)], "tensor", 1),
            (dst[0].at[pl.ds(local + half, half)], dst[0].at[pl.ds(3 * local + half, half)], "tensor", 2),
        ], 2, True)


def norm_back(own, low_parts, high_parts, tokens, cotangent, ln_gain):
    rows, model = tokens.shape
    tiles = 6
    tile = rows // tiles
    half = tiles // 2

    def inner(own_low, own_high, l0, l1, h0, h1, t_ref, c_ref, gain_ref, o_ref, s_ref):
        step = pl.program_id(0)

        def compute(a, b, c):
            grad = a[...].astype(f32) + b[...].astype(f32) + c[...].astype(f32)
            cot = c_ref[...].astype(f32)
            xhat, inverse = norm_parts(t_ref[...].astype(f32))
            scaled = grad * gain_ref[...]
            both = grad * xhat
            o_ref[...] = cot + inverse * (
                scaled
                - jnp.mean(scaled, axis=-1, keepdims=True)
                - xhat * jnp.mean(scaled * xhat, axis=-1, keepdims=True))
            terms = [jnp.sum(v.reshape(tile // 8, 8, model), axis=0) for v in (both, grad, cot)]

            @pl.when(step == 0)
            def _():
                for n in range(3):
                    s_ref[n] = terms[n]

            @pl.when(step > 0)
            def _():
                for n in range(3):
                    s_ref[n] += terms[n]

        @pl.when(step < half)
        def _():
            compute(own_low, l0, l1)

        @pl.when(step >= half)
        def _():
            compute(own_high, h0, h1)

    low = lambda i: (jnp.minimum(i, half - 1), 0)
    high = lambda i: (jnp.maximum(i - half, 0), 0)
    each = lambda i: (i, 0)
    block = (tile, model)
    (grad, sums), ignored = tiled(
        inner, (tiles,),
        [(own[0], block, low), (own[1], block, high)]
        + [(a, block, low) for a in low_parts] + [(a, block, high) for a in high_parts]
        + [(tokens, block, each), (cotangent, block, each), (ln_gain[None], (1, model), lambda i: (0, 0))],
        [((rows, model), f32, block, each), ((3, 8, model), f32, (3, 8, model), lambda i: (0, 0, 0))])
    return grad, jnp.sum(sums, axis=1)


def norm_parts(rows_in):
    row_mean = jnp.mean(rows_in, axis=-1, keepdims=True)
    centred = rows_in - row_mean
    inverse = lax.rsqrt(jnp.mean(centred * centred, axis=-1, keepdims=True) + norm_eps)
    return centred * inverse, inverse


def gelu_parts(v):
    scale = (2.0 / jnp.pi) ** 0.5
    square = v * v
    t = jnp.tanh(v * (scale + (scale * 0.044715) * square))
    half = 0.5 * (1.0 + t)
    slope = half + (half * (1.0 - t)) * (v * (scale + (scale * 3 * 0.044715) * square))
    return v * half, slope


def body(
    tokens,
    cotangent,
    ln_gain,
    ln_bias,
    w_qkv,
    b_qkv,
    w_out,
    w_fc1,
    b_fc1,
    w_fc2,
    resid_bias,
    parents,
):
    size = lax.axis_size("tensor")
    groups = lax.axis_size("dp")
    local_rows, model = tokens.shape
    me = lax.axis_index("tensor")
    width = w_qkv.shape[2]
    four = size == 4
    t1, t2 = ("tensor", 1), ("tensor", 2)
    half_cols = model // 2

    tables = rope_tables()
    up_w = lax.all_gather(w_fc1, "dp", axis=0, tiled=True)
    w_heads = jnp.concatenate([w_qkv, jnp.transpose(w_out)[None]], axis=0)
    heads_w = lax.all_gather(w_heads, "dp", axis=1, tiled=True)
    down_w = lax.all_gather(w_fc2, "dp", axis=1, tiled=True)
    if four:
        normed = norm_gather(tokens, ln_gain, ln_bias, 1)
    else:
        normed_local = (norm_parts(tokens.astype(f32))[0] * ln_gain + ln_bias).astype(bf16)
        normed, cot_full = (
            jnp.concatenate([x] + [xor_send(x, i, size) for i in range(1, size)], axis=0)
            for x in (normed_local, cotangent))
    activated, slope, got = hidden_forward(
        normed, up_w, b_fc1, local_rows, half_cols, gather_sides(cotangent, 2) if four else None)
    if four:
        cot_full = tiled(None, (), [], [], gather_corner(got[0], 3))[1][0]
    projected = (
        jnp.einsum(
            "td,cdh->cth", after(normed, activated, cot_full), heads_w[:3], preferred_element_type=f32)
        + b_qkv[:, None, :]
    ).astype(bf16)
    grad_w_fc2 = dot_tn(after(activated, projected), cot_full).astype(bf16)
    summed_fc2 = lax.psum_scatter(grad_w_fc2, "dp", scatter_dimension=1, tiled=True)
    grad_attended = dot_nn(after(cot_full, grad_w_fc2), heads_w[3]).astype(bf16)
    attended, grad_qkv, aux = attention(parents[0], me[None], size, *tables, projected, grad_attended)

    grad_w_out = dot_tn(attended, cot_full).astype(bf16)
    summed_out = lax.psum_scatter(grad_w_out, "dp", scatter_dimension=1, tiled=True)
    branch, ignored = chunk_matmul(
        [(after(attended, grad_w_out), heads_w, -1, 3), (activated, down_w, -1, None)],
        model, half_cols, size, size, lambda i: i, cut=2)
    grad_w_qkv, got = qkv_grads(
        after(normed, branch[0]), grad_qkv, half_cols,
        sending(4, (branch[6],) + t1, (branch[7],) + t2) if four else None)
    summed_qkv = lax.psum_scatter(grad_w_qkv, "dp", scatter_dimension=1, tiled=True)
    grad_hidden, sums_fc1, branch_next, side = hidden_grad(
        after(cot_full, grad_w_qkv), down_w, slope, local_rows, half_cols,
        sending(5, (branch[2],) + t1, (branch[5],) + t2) if four else None,
        [(branch[3], got[1]), (branch[4], got[0])] if four else [])
    dp_bits = range(1, groups)
    backs = [(grad_qkv, heads_w, c, c) for c in range(3)] + [(after(grad_hidden, summed_fc2), up_w, -1, -1)]
    if four:
        far, last = chunk_matmul(
            backs, model, half_cols, 8, 4, lambda i: 7 - i - 2 * (i // 3),
            sending(6, (branch_next[0],) + t1, (branch_next[1],) + t2))
        branch_sum = [
            branch[0].astype(f32) + side[0].astype(f32) + last[1].astype(f32),
            branch[1].astype(f32) + last[0].astype(f32) + side[1].astype(f32)]
        grad_w_fc1, got = weight_grad(
            after(normed, far[7], summed_out), grad_hidden, half_cols, half_cols,
            sending(
                7, (far[6],) + t1, (far[7],) + t2,
                *[(aux, "dp", bits) for bits in dp_bits], *[(sums_fc1, "dp", bits) for bits in dp_bits]))
        all_aux = [aux] + got[2 : 1 + groups]
        all_fc1 = [sums_fc1] + got[1 + groups :]
        backs[3] = (after(grad_hidden, grad_w_fc1),) + backs[3][1:]
        near, side = chunk_matmul(
            backs, model, half_cols, 8, 4, lambda i: 4 - i - i // 2,
            sending(8, (far[2],) + t1, (far[5],) + t2), {3: got[1], 4: got[0]})
        one, two = xor_send(near[3], 1, size), xor_send(near[4], 2, size)
        input_grad, terms = norm_back(
            [near[0], near[1]], [side[0], two], [one, side[1]], tokens, cotangent, ln_gain)
        branch_sum[0] = after(branch_sum[0], near[0])
        all_aux[0] = after(aux, near[0])
        all_fc1[0] = after(sums_fc1, near[0])
        summed_qkv, summed_out, summed_fc2 = lax.optimization_barrier((summed_qkv, summed_out, summed_fc2, near[0]))[:3]
    else:
        parts, ignored = chunk_matmul(backs, model, half_cols, size, size, lambda i: i, cut=2)
        grad_w_fc1, ignored = weight_grad(normed, grad_hidden, half_cols, half_cols, None)
        all_aux, all_fc1 = (list(lax.all_gather(x, "dp")) for x in (aux, sums_fc1))
        branch_sum = scatter_rest(branch, size)
        grad_normed = jnp.concatenate(scatter_rest(parts, size), axis=0)
        xhat, inverse = norm_parts(tokens.astype(f32))
        grad_xhat = grad_normed * ln_gain
        cot_local = cotangent.astype(f32)
        input_grad = cot_local + inverse * (
            grad_xhat
            - jnp.mean(grad_xhat, axis=-1, keepdims=True)
            - xhat * jnp.mean(grad_xhat * xhat, axis=-1, keepdims=True)
        )
        terms = jnp.stack(
            [jnp.sum(grad_normed * xhat, axis=0), jnp.sum(grad_normed, axis=0), jnp.sum(cot_local, axis=0)]
        )
    summed_fc1 = lax.psum_scatter(grad_w_fc1, "dp", scatter_dimension=0, tiled=True)
    output_rows = (
        tokens.astype(f32) + jnp.concatenate(branch_sum, axis=0) + resid_bias).astype(bf16)
    summed_fc1, summed_qkv, summed_out, summed_fc2 = (
        w.astype(f32) for w in (summed_fc1, summed_qkv, summed_out, summed_fc2))

    bias_qkv = jnp.transpose(sum(a[:, :3] for a in all_aux), (1, 0, 2)).reshape(3, width)
    bias_fc1 = jnp.sum(sum(all_fc1), axis=0)
    head_top = functools.reduce(jnp.maximum, [a[:, 3:5, 0] for a in all_aux]).reshape(-1)
    factor = jnp.sqrt(clip_tau / jnp.maximum(head_top, clip_tau))
    clipped_qk = (w_qkv[:2].astype(f32) * jnp.repeat(factor, HDIM)[None, None, :]).astype(bf16)

    every = size * groups
    pieces = jnp.transpose(terms.reshape(3, every, model // every), (1, 0, 2)).reshape(every, -1)
    pieces = lax.all_to_all(pieces, ("dp", "tensor"), 0, 0, tiled=True)
    grad_small = jnp.sum(pieces, axis=0).reshape(3, model // every)
    return (
        output_rows,
        input_grad,
        grad_small,
        summed_qkv,
        bias_qkv,
        summed_out,
        summed_fc1,
        bias_fc1,
        summed_fc2,
        clipped_qk,
    )


def solution(mesh):
    return jax.shard_map(
        body,
        mesh=mesh,
        in_specs=(
            P(("dp", "tensor"), None),
            P(("dp", "tensor"), None),
            P(),
            P(),
            P(None, "dp", "tensor"),
            P(None, "tensor"),
            P("tensor", "dp"),
            P("dp", "tensor"),
            P("tensor"),
            P("tensor", "dp"),
            P(),
            P("dp", None),
        ),
        out_specs=(
            P(("dp", "tensor"), None),
            P(("dp", "tensor"), None),
            P(None, ("dp", "tensor")),
            P(None, "dp", "tensor"),
            P(None, "tensor"),
            P("tensor", "dp"),
            P("dp", "tensor"),
            P("tensor"),
            P("tensor", "dp"),
            P(None, "dp", "tensor"),
        ),
        check_vma=False,
    )
```
